32 devices in a mesh: dp: 16 (over z, x, core), tensor: 2 (over y).
Axes of the slice: x: 2, y: 2, z: 4, core: 2. Of those that a mesh axis runs over, the one named last changes fastest.
Arguments:
- inputs: bfloat16 [16, 256, 1024], P('dp'), may hold values from -6 to 6
- cotangent: bfloat16 [16, 256, 1024], P('dp'), may hold values from -6 to 6
- lengths: int32 [16], P('dp'), may hold values from 16 to 256, as said below
- norm1_gain: float32 [1024], replicated, may hold values from 0.5 to 1.5
- w_query: bfloat16 [1024, 1024], P(None, 'tensor'), may hold values from -0.1875 to 0.1875
- w_key: bfloat16 [1024, 1024], P(None, 'tensor'), may hold values from -0.1875 to 0.1875
- w_value: bfloat16 [1024, 2048], P(None, 'tensor'), may hold values from -0.1875 to 0.1875
- w_gate: bfloat16 [1024, 2048], P(None, 'tensor'), may hold values from -0.1875 to 0.1875
- w_alpha: bfloat16 [1024, 8], P(None, 'tensor'), may hold values from -0.1875 to 0.1875
- w_beta: bfloat16 [1024, 8], P(None, 'tensor'), may hold values from -0.1875 to 0.1875
- conv_query: float32 [4, 1024], P(None, 'tensor'), may hold values from -3 to 3
- conv_key: float32 [4, 1024], P(None, 'tensor'), may hold values from -3 to 3
- conv_value: float32 [4, 2048], P(None, 'tensor'), may hold values from -3 to 3
- a_log: float32 [8], P('tensor'), may hold values from -7 to -2.5
- dt_bias: float32 [8], P('tensor'), may hold values from -4 to 1
- onorm_gain: float32 [256], replicated, may hold values from 0.5 to 1.5
- w_out: bfloat16 [2048, 1024], P('tensor'), may hold values from -0.25 to 0.25
- norm2_gain: float32 [1024], replicated, may hold values from 0.5 to 1.5
- w_one: bfloat16 [1024, 2816], P(None, 'tensor'), may hold values from -0.1875 to 0.1875
- w_three: bfloat16 [1024, 2816], P(None, 'tensor'), may hold values from -0.1875 to 0.1875
- w_two: bfloat16 [2816, 1024], P('tensor'), may hold values from -0.15625 to 0.15625
Outputs:
- outputs: float32 [16, 256, 1024], P('dp')
- in_grad: float32 [16, 256, 1024], P('dp')
- grad_norm1_gain: float32 [1024], replicated
- grad_w_query: float32 [1024, 1024], P('dp', 'tensor')
- grad_w_key: float32 [1024, 1024], P('dp', 'tensor')
- grad_w_value: float32 [1024, 2048], P('dp', 'tensor')
- grad_w_gate: float32 [1024, 2048], P('dp', 'tensor')
- grad_w_alpha: float32 [1024, 8], P('dp', 'tensor')
- grad_w_beta: float32 [1024, 8], P('dp', 'tensor')
- grad_conv_query: float32 [4, 1024], P(None, 'tensor')
- grad_conv_key: float32 [4, 1024], P(None, 'tensor')
- grad_conv_value: float32 [4, 2048], P(None, 'tensor')
- grad_a_log: float32 [8], P('tensor')
- grad_dt_bias: float32 [8], P('tensor')
- grad_onorm_gain: float32 [256], replicated
- grad_w_out: float32 [2048, 1024], P('tensor', 'dp')
- grad_norm2_gain: float32 [1024], replicated
- grad_w_one: float32 [1024, 2816], P('dp', 'tensor')
- grad_w_three: float32 [1024, 2816], P('dp', 'tensor')
- grad_w_two: float32 [2816, 1024], P('tensor', 'dp')
The draws below stay inside these ranges and needn't reach their ends.
Inputs may be any that keep to these rules, and one draw needn't show every extreme that they name: Each slot holds one sequence from position 0; positions from lengths[s] on are padding. Slot 0 always holds a sequence of 256 positions; the slots of one index of dp share a drawn upper limit, so loads differ between devices.
All inputs are finite; a program needn't handle non-finite values.
Results may differ from the reference program's by a relative error of at most 0.02.
Values sent between devices are 32-bit elements; how exact they have to be, the bound alone decides.
No kernel may reach another device: no remote copies, remote signals or barrier semaphores. Data moves between devices by JAX's collectives and lax.ppermute only.
A program may use at most 256 MiB of HBM per device.

```python
import jax
import jax.numpy as jnp
from jax import lax

D = 1024
H = 8
DK = 128
DV = 256
FF = 2816
KC = 4
BLK = 64
SEQ_LEN = 256
SEQ_DEV = 1
SEQS = 16


def draw_lengths(key, part):
    cap_key, pick_key = jax.random.split(key)
    device_count = SEQS // SEQ_DEV
    dev_caps = jax.random.randint(cap_key, (device_count, 1), SEQ_LEN // 8, SEQ_LEN + 1)
    lower_cap = dev_caps // 2
    random_bits = jax.random.randint(pick_key, (device_count, SEQ_DEV), 0, 1 << 20)
    drawn = lower_cap + random_bits % (dev_caps - lower_cap + 1)
    drawn = drawn.reshape(SEQS).astype(jnp.int32)
    return drawn.at[0].set(SEQ_LEN)


def spiked(result, rng, source, target, shards_of, factor):
    def block_of(axis_at):
        return (jnp.arange(result.shape[axis_at]) // (result.shape[axis_at] // shards_of)).reshape((-1,) + (1,) * (result.ndim - 1 - axis_at))

    one_side = jax.random.permutation(rng, shards_of)[block_of(target)]
    other_side = (block_of(target) + shards_of // 2) % shards_of
    return jnp.where((block_of(source) == one_side) | (block_of(source) == other_side), factor * result, result)


def level_of(stream_key, extent, cuts, smallest, high):
    gain = 1.0
    for axis_at, parts in cuts:
        steps = jax.random.uniform(jax.random.fold_in(jax.random.fold_in(stream_key, 6), axis_at), (parts,), jnp.float32, smallest / len(cuts), high / len(cuts))
        gain = gain * jnp.repeat(jnp.exp(steps), extent[axis_at] // parts).reshape((-1,) + (1,) * (len(extent) - 1 - axis_at))
    return gain


def centred(key, extent, scale, limit, cuts=(), held_as=jnp.bfloat16):
    entries = jax.random.normal(key, extent, jnp.float32) * scale
    if len(cuts) > 0:
        entries = level_of(key, extent, cuts, -0.22, 0.18) * entries
    return jnp.clip(entries, min=-limit, max=limit).astype(held_as)


def bell_draw_with(stream_key, extent, scale, reach, cuts, heavy, held_as=jnp.bfloat16):
    array = scale * jax.random.normal(stream_key, extent, jnp.float32)
    if cuts:
        array = array * level_of(stream_key, extent, cuts, -0.22, 0.18)
    return jnp.clip(spiked(array, jax.random.fold_in(stream_key, 3), *heavy), -reach, reach).astype(held_as)


def setup_inputs(seed: int = 0) -> dict:
    arg_keys = jax.random.split(jax.random.key(seed), 22)
    return {
        "inputs": bell_draw_with(arg_keys[0], (SEQS, SEQ_LEN, D), 1.0, 6.0, ((0, 16),), (0, 2, 16, 2.0)),
        "cotangent": bell_draw_with(arg_keys[1], (SEQS, SEQ_LEN, D), 1.0, 6.0, ((0, 16),), (0, 2, 16, 2.0)),
        "lengths": draw_lengths(jax.random.fold_in(arg_keys[21], 71), 0),
        "norm1_gain": jnp.clip(1.0 + 0.1 * jax.random.normal(arg_keys[3], (D,), jnp.float32), 0.5, 1.5),
        "w_query": centred(arg_keys[4], (D, H * DK), D ** -0.5, 0.1875, ((1, 2),)),
        "w_key": centred(arg_keys[5], (D, H * DK), D ** -0.5, 0.1875, ((1, 2),)),
        "w_value": centred(arg_keys[6], (D, H * DV), D ** -0.5, 0.1875, ((1, 2),)),
        "w_gate": centred(arg_keys[7], (D, H * DV), D ** -0.5, 0.1875, ((1, 2),)),
        "w_alpha": centred(arg_keys[8], (D, H), D ** -0.5, 0.1875, ((1, 2),)),
        "w_beta": centred(arg_keys[9], (D, H), D ** -0.5, 0.1875, ((1, 2),)),
        "conv_query": centred(arg_keys[10], (KC, H * DK), 0.5, 3.0, ((1, 2),), jnp.float32),
        "conv_key": centred(arg_keys[11], (KC, H * DK), 0.5, 3.0, ((1, 2),), jnp.float32),
        "conv_value": centred(arg_keys[12], (KC, H * DV), 0.5, 3.0, ((1, 2),), jnp.float32),
        "a_log": jnp.clip(-7.0 + 4.5 * jax.random.uniform(arg_keys[13], (H,), jnp.float32) ** level_of(arg_keys[13], (H,), ((0, 2),), -0.2, 0.2), -7.0, -2.5),
        "dt_bias": jnp.clip(-4.0 + 5.0 * jax.random.uniform(arg_keys[14], (H,), jnp.float32) ** level_of(arg_keys[14], (H,), ((0, 2),), -0.2, 0.2), -4.0, 1.0),
        "onorm_gain": jnp.clip(1.0 + 0.1 * jax.random.normal(arg_keys[15], (DV,), jnp.float32), 0.5, 1.5),
        "w_out": centred(arg_keys[16], (H * DV, D), (H * DV // 4) ** -0.5, 0.25, ((0, 2),)),
        "norm2_gain": jnp.clip(1.0 + 0.1 * jax.random.normal(arg_keys[17], (D,), jnp.float32), 0.5, 1.5),
        "w_one": centred(arg_keys[18], (D, FF), D ** -0.5, 0.1875, ((1, 2),)),
        "w_three": centred(arg_keys[19], (D, FF), D ** -0.5, 0.1875, ((1, 2),)),
        "w_two": centred(arg_keys[20], (FF, D), (FF // 2) ** -0.5, 0.15625, ((0, 2),)),
    }


epsilon = 1e-06
highest = lax.Precision.HIGHEST

def rms_scale(rows_in, gain_in):
    return rows_in * lax.rsqrt(lax.optimization_barrier(jnp.mean(rows_in * rows_in, axis=-1, keepdims=True)) + epsilon) * gain_in

def matmul_nt(first_arr, second_arr):
    return lax.dot_general(first_arr.astype(jnp.float32), second_arr.astype(jnp.float32), (((1,), (1,)), ((), ())), preferred_element_type=jnp.float32)

def matmul_tn(first_arr, second_arr):
    return lax.dot_general(first_arr.astype(jnp.float32), second_arr.astype(jnp.float32), (((0,), (0,)), ((), ())), preferred_element_type=jnp.float32)

def causal_conv(series, kernel):
    kernel_len = kernel.shape[0]
    length = series.shape[0]
    padded = jnp.pad(series, ((kernel_len - 1, 0), (0, 0)))
    summed = kernel[0] * padded[0:length]
    for tap_idx in range(1, kernel_len):
        summed = summed + kernel[tap_idx] * padded[tap_idx:tap_idx + length]
    return summed

def arrange(source, block_len):
    seq_len = source.shape[0]
    shaped = source.reshape((seq_len // block_len, block_len) + source.shape[1:])
    return jnp.transpose(shaped, (2, 0, 1) + tuple(range(3, shaped.ndim)))

def delta_blocks(queries, keys_all, values, beta_vals, decays):
    seq_len, head_count, key_dim = queries.shape
    val_dim = values.shape[2]
    data_type = queries.dtype
    q_blocks = arrange(queries, BLK)
    k_blocks = arrange(keys_all, BLK)
    v_blocks = arrange(values, BLK)
    beta_blk = arrange(beta_vals, BLK)
    cum_decay = jnp.cumsum(arrange(decays, BLK), axis=-1)
    row_pos = lax.broadcasted_iota(jnp.int32, (BLK, BLK), 0)
    col_pos = lax.broadcasted_iota(jnp.int32, (BLK, BLK), 1)
    inclusive = (row_pos >= col_pos).astype(data_type)
    strict = (row_pos > col_pos).astype(data_type)
    differ = cum_decay[..., :, None] - cum_decay[..., None, :]
    within = jnp.exp(jnp.where(row_pos >= col_pos, differ, jnp.zeros_like(differ))) * inclusive
    key_key = jnp.einsum('hnck,hnsk->hncs', k_blocks, k_blocks, precision=highest)
    system = jnp.eye(BLK, dtype=data_type) + beta_blk[..., :, None] * key_key * within * strict
    new_vals = jax.scipy.linalg.solve_triangular(system, beta_blk[..., None] * v_blocks, lower=True, unit_diagonal=True)
    new_keys = jax.scipy.linalg.solve_triangular(system, (beta_blk * jnp.exp(cum_decay))[..., None] * k_blocks, lower=True, unit_diagonal=True)
    query_key = jnp.einsum('hnck,hnsk->hncs', q_blocks, k_blocks, precision=highest) * within
    q_decay = q_blocks * jnp.exp(cum_decay)[..., None]
    last_decay = cum_decay[..., -1]
    k_decay = k_blocks * jnp.exp(last_decay[..., None] - cum_decay)[..., None]

    def advance(memory, pieces):
        vals_in, keys_in, scores, query_dec, key_dec, decay_end = pieces
        corrected = vals_in - jnp.einsum('hck,hvk->hcv', keys_in, memory, precision=highest)
        output = jnp.einsum('hck,hvk->hcv', query_dec, memory, precision=highest) + jnp.einsum('hcs,hsv->hcv', scores, corrected, precision=highest)
        memory = jnp.exp(decay_end)[:, None, None] * memory + jnp.einsum('hsv,hsk->hvk', corrected, key_dec, precision=highest)
        return (memory, output)
    start_memory = jnp.zeros((head_count, val_dim, key_dim), data_type)
    stacked = tuple((jnp.moveaxis(source, 1, 0) for source in (new_vals, new_keys, query_key, q_decay, k_decay, last_decay)))
    final_memory, outputs = lax.scan(advance, start_memory, stacked)
    outputs = jnp.transpose(outputs, (0, 2, 1, 3))
    return outputs.reshape(seq_len, head_count, val_dim)

def gated_mixer(q_raw, k_raw, v_raw, g_raw, a_raw, b_raw, conv_q, conv_k, conv_v, log_rate, bias_rate, out_gain):
    seq_len = q_raw.shape[0]
    head_count = a_raw.shape[1]
    key_dim = q_raw.shape[1] // head_count
    val_dim = v_raw.shape[1] // head_count
    queries = jax.nn.silu(causal_conv(q_raw, conv_q)).reshape(seq_len, head_count, key_dim)
    keys_all = jax.nn.silu(causal_conv(k_raw, conv_k)).reshape(seq_len, head_count, key_dim)
    values = jax.nn.silu(causal_conv(v_raw, conv_v)).reshape(seq_len, head_count, val_dim)
    queries = queries * lax.rsqrt(lax.optimization_barrier(jnp.sum(queries * queries, axis=-1, keepdims=True)) + epsilon) * key_dim ** (-0.5)
    keys_all = keys_all * lax.rsqrt(lax.optimization_barrier(jnp.sum(keys_all * keys_all, axis=-1, keepdims=True)) + epsilon)
    beta_vals = jax.nn.sigmoid(b_raw)
    decays = -jnp.exp(log_rate) * jax.nn.softplus(a_raw + bias_rate)
    mixed = delta_blocks(queries, keys_all, values, beta_vals, decays)
    mixed = mixed * lax.rsqrt(lax.optimization_barrier(jnp.mean(mixed * mixed, axis=-1, keepdims=True)) + epsilon) * out_gain
    gate_act = jax.nn.silu(g_raw.reshape(seq_len, head_count, val_dim))
    return (mixed * gate_act).reshape(seq_len, head_count * val_dim)

def run_mixer(q_in, k_in, v_in, g_in, a_in, b_in, conv_q, conv_k, conv_v, log_rate, bias_rate, out_gain):
    per_sequence = jax.vmap(gated_mixer, in_axes=(0, 0, 0, 0, 0, 0, None, None, None, None, None, None))
    return per_sequence(q_in, k_in, v_in, g_in, a_in, b_in, conv_q, conv_k, conv_v, log_rate, bias_rate, out_gain)

def reference(inputs, cotangent, lengths, norm1_gain, w_query, w_key, w_value, w_gate, w_alpha, w_beta, conv_query, conv_key, conv_value, a_log, dt_bias, onorm_gain, w_out, norm2_gain, w_one, w_three, w_two):
    group_count = SEQS // SEQ_DEV
    matrices = (w_query, w_key, w_value, w_gate, w_alpha, w_beta)
    params_all = (norm1_gain, w_query, w_key, w_value, w_gate, w_alpha, w_beta, conv_query, conv_key, conv_value, a_log, dt_bias, onorm_gain, w_out, norm2_gain, w_one, w_three, w_two)

    def one_group(totals, pieces):
        x_block, cot_block, len_block = pieces
        seq_count = x_block.shape[0]
        row_count = seq_count * SEQ_LEN
        positions = lax.broadcasted_iota(jnp.int32, (seq_count, SEQ_LEN), 1)
        live_rows = (positions < len_block.astype(jnp.int32)[:, None]).astype(jnp.float32).reshape(row_count, 1)
        x_rows = x_block.reshape(row_count, D).astype(jnp.float32)
        h_one = rms_scale(x_rows, norm1_gain).astype(jnp.bfloat16)
        raw_proj = tuple((jnp.dot(h_one.astype(jnp.float32), matrix.astype(jnp.float32), preferred_element_type=jnp.float32).astype(jnp.bfloat16) for matrix in matrices))
        mixer_in = tuple((raw_arr.astype(jnp.float32).reshape(seq_count, SEQ_LEN, -1) for raw_arr in raw_proj))
        gated_full, mixer_back = jax.vjp(run_mixer, *mixer_in, conv_query, conv_key, conv_value, a_log, dt_bias, onorm_gain)
        gated_out = gated_full.reshape(row_count, -1).astype(jnp.bfloat16)
        x_mid = x_rows + jnp.dot(gated_out.astype(jnp.float32), w_out.astype(jnp.float32), preferred_element_type=jnp.float32)
        h_two = rms_scale(x_mid, norm2_gain).astype(jnp.bfloat16)
        pre_one = jnp.dot(h_two.astype(jnp.float32), w_one.astype(jnp.float32), preferred_element_type=jnp.float32)
        pre_three = jnp.dot(h_two.astype(jnp.float32), w_three.astype(jnp.float32), preferred_element_type=jnp.float32)
        sig_one = jax.nn.sigmoid(pre_one)
        hidden = (pre_one * sig_one * pre_three).astype(jnp.bfloat16)
        outputs = (x_mid + jnp.dot(hidden.astype(jnp.float32), w_two.astype(jnp.float32), preferred_element_type=jnp.float32)) * live_rows
        grad_out = cot_block.reshape(row_count, D).astype(jnp.float32) * live_rows
        grad_out_b = grad_out.astype(jnp.bfloat16)
        d_hidden = matmul_nt(grad_out_b, w_two)
        d_pre_one = (d_hidden * pre_three * sig_one * (1.0 + pre_one * (1.0 - sig_one))).astype(jnp.bfloat16)
        d_pre_three = (d_hidden * pre_one * sig_one).astype(jnp.bfloat16)
        d_h_two = matmul_nt(d_pre_one, w_one) + matmul_nt(d_pre_three, w_three)
        norm2_value, norm2_back = jax.vjp(rms_scale, x_mid, norm2_gain)
        d_mid_part, grad_norm2 = norm2_back(d_h_two)
        d_x_mid = grad_out + d_mid_part
        d_mid_b = d_x_mid.astype(jnp.bfloat16)
        d_gated = matmul_nt(d_mid_b, w_out)
        mixer_grads = mixer_back(d_gated.reshape(seq_count, SEQ_LEN, -1))
        d_raw = tuple((grad_arr.reshape(row_count, -1).astype(jnp.bfloat16) for grad_arr in mixer_grads[:6]))
        d_h_one = matmul_nt(d_raw[0], matrices[0])
        for index_w in range(1, 6):
            d_h_one = d_h_one + matmul_nt(d_raw[index_w], matrices[index_w])
        norm1_value, norm1_back = jax.vjp(rms_scale, x_rows, norm1_gain)
        d_in_part, grad_norm1 = norm1_back(d_h_one)
        in_grad = d_x_mid + d_in_part
        grad_mats = tuple((matmul_tn(h_one, d_arr) for d_arr in d_raw))
        fresh_terms = (grad_norm1,) + grad_mats + tuple(mixer_grads[6:12]) + (matmul_tn(gated_out, d_mid_b), grad_norm2, matmul_tn(h_two, d_pre_one), matmul_tn(h_two, d_pre_three), matmul_tn(hidden, grad_out_b))
        new_totals = jax.tree.map(jnp.add, totals, fresh_terms)
        return (new_totals, (outputs.reshape(seq_count, SEQ_LEN, D), in_grad.reshape(seq_count, SEQ_LEN, D)))
    start_totals = tuple((jnp.zeros(param.shape, jnp.float32) for param in params_all))
    stacked = (inputs.reshape(group_count, SEQ_DEV, SEQ_LEN, D), cotangent.reshape(group_count, SEQ_DEV, SEQ_LEN, D), lengths.reshape(group_count, SEQ_DEV))
    totals, (out_all, grad_all) = lax.scan(one_group, start_totals, stacked)
    out_all = out_all.reshape(SEQS, SEQ_LEN, D)
    grad_all = grad_all.reshape(SEQS, SEQ_LEN, D)
    return (out_all, grad_all, totals[0], totals[1], totals[2], totals[3], totals[4], totals[5], totals[6], totals[7], totals[8], totals[9], totals[10], totals[11], totals[12], totals[13], totals[14], totals[15], totals[16], totals[17])
```

```python
import functools
import math

import jax
import jax.numpy as jnp
from jax import lax
from jax.experimental import pallas as pl
from jax.experimental.pallas import tpu as pltpu
from jax.sharding import PartitionSpec as P

epsilon = 1e-06
f32 = jnp.float32
bf16 = jnp.bfloat16
CHUNK = 128
LANES = 128


def rms_scale(rows_in, gain_in):
    return (
        rows_in * lax.rsqrt(jnp.mean(rows_in * rows_in, axis=-1, keepdims=True) + epsilon) * gain_in
    )


def matmul_nt(first_arr, second_arr):
    return lax.dot_general(
        first_arr, second_arr, (((1,), (1,)), ((), ())), preferred_element_type=f32
    )


def mm(first_arr, second_arr, first_dim=1, second_dim=0):
    return lax.dot_general(
        first_arr,
        second_arr,
        (((first_dim,), (second_dim,)), ((), ())),
        precision=lax.Precision.HIGHEST,
        preferred_element_type=f32,
    )


def delayed(series, steps):
    if steps == 0:
        return series
    rows = lax.broadcasted_iota(jnp.int32, series.shape, 0)
    return jnp.where(rows >= steps, pltpu.roll(series, steps, 0), 0.0)


def advanced(series, steps):
    if steps == 0:
        return series
    length = series.shape[0]
    rows = lax.broadcasted_iota(jnp.int32, series.shape, 0)
    return jnp.where(rows < length - steps, pltpu.roll(series, length - steps, 0), 0.0)


def conv_of(series, taps):
    count = taps.shape[0]
    total = taps[count - 1 : count] * series
    for tap in range(count - 1):
        total = total + taps[tap : tap + 1] * delayed(series, count - 1 - tap)
    return total


def conv_back(series, taps, cotangent):
    count = taps.shape[0]
    d_series = taps[count - 1 : count] * cotangent
    d_taps = []
    for tap in range(count):
        steps = count - 1 - tap
        if steps > 0:
            d_series = d_series + taps[tap : tap + 1] * advanced(cotangent, steps)
        d_taps.append(jnp.sum(cotangent * delayed(series, steps), axis=0, keepdims=True))
    return d_series, d_taps


def silu_slope(value, sig):
    return sig * (1.0 + value * (1.0 - sig))


def unit_back(act, norm, cotangent, scale):
    inner = jnp.sum(cotangent * act, axis=1, keepdims=True)
    return scale * (norm * cotangent - act * (norm * norm * norm * inner))


class Grid2:
    def __init__(self, length):
        row = lax.broadcasted_iota(jnp.int32, (length, length), 0)
        col = lax.broadcasted_iota(jnp.int32, (length, length), 1)
        self.row, self.col = row, col
        self.lower = row >= col
        self.strict = row > col
        self.upper = row <= col
        self.eye = row == col

    def to_row(self, column):
        return jnp.sum(jnp.where(self.eye, column, 0.0), axis=0, keepdims=True)


def head_terms(h, heads, q_ref, k_ref, v_ref, ab_ref, cq_ref, ck_ref, cv_ref, rate_ref, bias_ref, grid2):
    dk = q_ref.shape[1] // heads
    dv = v_ref.shape[1] // heads
    ks, vs = slice(h * dk, (h + 1) * dk), slice(h * dv, (h + 1) * dv)
    t = {}
    t["q_raw"], t["k_raw"] = q_ref[:, ks].astype(f32), k_ref[:, ks].astype(f32)
    t["v_raw"] = v_ref[:, vs].astype(f32)
    for name, conv_ref, cols in (("q", cq_ref, ks), ("k", ck_ref, ks), ("v", cv_ref, vs)):
        pre = conv_of(t[name + "_raw"], conv_ref[:, cols])
        sig = jax.nn.sigmoid(pre)
        t[name + "_pre"], t[name + "_sig"], t[name + "_act"] = pre, sig, pre * sig
    for name in ("q", "k"):
        act = t[name + "_act"]
        t[name + "_norm"] = lax.rsqrt(jnp.sum(act * act, axis=1, keepdims=True) + epsilon)
    t["q"] = t["q_act"] * t["q_norm"] * dk ** (-0.5)
    t["k"] = t["k_act"] * t["k_norm"]
    t["v"] = t["v_act"]
    ab = ab_ref[...].astype(f32)
    t["beta"] = jax.nn.sigmoid(ab[:, heads + h : heads + h + 1])
    z = ab[:, h : h + 1] + bias_ref[:, h : h + 1]
    t["z"] = z
    t["rate"] = -jnp.exp(rate_ref[:, h : h + 1])
    t["decay"] = t["rate"] * (jnp.maximum(z, 0.0) + jnp.log1p(jnp.exp(-jnp.abs(z))))
    decay_row = grid2.to_row(t["decay"])
    cum_col = jnp.sum(jnp.where(grid2.lower, decay_row, 0.0), axis=1, keepdims=True)
    cum_row = jnp.sum(jnp.where(grid2.upper, t["decay"], 0.0), axis=0, keepdims=True)
    differ = jnp.where(grid2.lower, cum_col - cum_row, 0.0)
    t["within"] = jnp.where(grid2.lower, jnp.exp(differ), 0.0)
    t["kk"] = jnp.where(grid2.strict, mm(t["k"], t["k"], 1, 1), 0.0) * t["within"]
    t["system"] = t["beta"] * t["kk"]
    t["scores"] = mm(t["q"], t["k"], 1, 1) * t["within"]
    return t


def unit_lower_inverses(blocks):
    size = blocks[0].shape[0]
    row = lax.broadcasted_iota(jnp.int32, (size, size), 0)
    col = lax.broadcasted_iota(jnp.int32, (size, size), 1)
    eye = jnp.where(row == col, 1.0, 0.0)
    half = 1
    found = None
    while half < size:
        pair = (row // (2 * half) == col // (2 * half)) & (row // half != col // half)
        parts = [jnp.where(pair, block, 0.0) for block in blocks]
        if found is None:
            found = [eye - part for part in parts]
        else:
            left = [mm(inv, part) for inv, part in zip(found, parts)]
            found = [inv - mm(lhs, inv) for inv, lhs in zip(found, left)]
        half *= 2
    return found


def forward_kernel(
    heads,
    q_ref,
    k_ref,
    v_ref,
    g_ref,
    ab_ref,
    cq_ref,
    ck_ref,
    cv_ref,
    rate_ref,
    bias_ref,
    gain_ref,
    gated_ref,
    inv_ref,
    new_ref,
    out_ref,
    system_ref,
    scores_ref,
):
    length = q_ref.shape[0]
    dv = v_ref.shape[1] // heads
    chunk = min(CHUNK, length)
    blocks = length // chunk
    grid2 = Grid2(length)
    for h in range(heads):
        t = head_terms(h, heads, q_ref, k_ref, v_ref, ab_ref, cq_ref, ck_ref, cv_ref, rate_ref, bias_ref, grid2)
        system_ref[h] = t["system"]
        scores_ref[h] = t["scores"]
        new_ref[:, h * dv : (h + 1) * dv] = t["beta"] * t["v"]
    found = unit_lower_inverses(
        [
            system_ref[h, b * chunk : (b + 1) * chunk, b * chunk : (b + 1) * chunk]
            for h in range(heads)
            for b in range(blocks)
        ]
    )
    for index, inv in enumerate(found):
        inv_ref[0, index] = inv
    for b in range(blocks):
        rows = slice(b * chunk, (b + 1) * chunk)
        for h in range(heads):
            cols = slice(h * dv, (h + 1) * dv)
            rhs = new_ref[rows, cols]
            if b > 0:
                rhs = rhs - mm(system_ref[h, rows, : b * chunk], new_ref[: b * chunk, cols])
            new_ref[rows, cols] = mm(found[h * blocks + b], rhs)
    gain = gain_ref[...]
    for h in range(heads):
        cols = slice(h * dv, (h + 1) * dv)
        out = mm(scores_ref[h], new_ref[:, cols])
        out_ref[:, cols] = out
        scaled = out * lax.rsqrt(jnp.mean(out * out, axis=1, keepdims=True) + epsilon) * gain
        gate = g_ref[:, cols].astype(f32)
        gated_ref[:, cols] = (scaled * (gate * jax.nn.sigmoid(gate))).astype(bf16)


def backward_kernel(
    heads,
    q_ref,
    k_ref,
    v_ref,
    g_ref,
    ab_ref,
    cq_ref,
    ck_ref,
    cv_ref,
    rate_ref,
    bias_ref,
    gain_ref,
    inv_ref,
    new_ref,
    out_ref,
    d_gated_ref,
    dq_ref,
    dk_ref,
    dv_ref,
    dg_ref,
    dab_ref,
    dcq_ref,
    dck_ref,
    dcv_ref,
    dsmall_ref,
    dgain_ref,
):
    length = q_ref.shape[0]
    dkey = q_ref.shape[1] // heads
    dval = v_ref.shape[1] // heads
    chunk = min(CHUNK, length)
    blocks = length // chunk
    grid2 = Grid2(length)
    first = pl.program_id(0) == 0

    @pl.when(first)
    def _():
        for ref in (dcq_ref, dck_ref, dcv_ref, dsmall_ref, dgain_ref):
            ref[...] = jnp.zeros_like(ref)

    gain = gain_ref[...]
    d_gain = jnp.zeros_like(gain)
    ab_lane = lax.broadcasted_iota(jnp.int32, dab_ref.shape, 1)
    d_ab = jnp.zeros(dab_ref.shape, f32)
    small_row = lax.broadcasted_iota(jnp.int32, dsmall_ref.shape, 0)
    small_lane = lax.broadcasted_iota(jnp.int32, dsmall_ref.shape, 1)
    d_small = jnp.zeros(dsmall_ref.shape, f32)
    for h in range(heads):
        ks, vs = slice(h * dkey, (h + 1) * dkey), slice(h * dval, (h + 1) * dval)
        t = head_terms(h, heads, q_ref, k_ref, v_ref, ab_ref, cq_ref, ck_ref, cv_ref, rate_ref, bias_ref, grid2)
        q, k, v, beta, within = t["q"], t["k"], t["v"], t["beta"], t["within"]
        new, out = new_ref[:, vs], out_ref[:, vs]
        d_gated = d_gated_ref[:, vs]
        gate = g_ref[:, vs].astype(f32)
        gate_sig = jax.nn.sigmoid(gate)
        norm = lax.rsqrt(jnp.mean(out * out, axis=1, keepdims=True) + epsilon)
        unit = out * norm
        dg_ref[:, vs] = (d_gated * unit * gain * silu_slope(gate, gate_sig)).astype(bf16)
        d_scaled = d_gated * (gate * gate_sig)
        d_gain = d_gain + jnp.sum(d_scaled * unit, axis=0, keepdims=True)
        d_unit = d_scaled * gain
        inner = jnp.mean(d_unit * unit, axis=1, keepdims=True)
        d_out = norm * (d_unit - unit * inner)
        d_new = mm(t["scores"], d_out, 0, 0)
        d_scores = mm(d_out, new, 1, 1)
        solved = [None] * blocks
        for b in reversed(range(blocks)):
            rows = slice(b * chunk, (b + 1) * chunk)
            rhs = d_new[rows]
            for later in range(b + 1, blocks):
                part = t["system"][later * chunk : (later + 1) * chunk, rows]
                rhs = rhs - mm(part, solved[later], 0, 0)
            solved[b] = mm(inv_ref[0, h * blocks + b], rhs, 0, 0)
        y = jnp.concatenate(solved, axis=0)
        d_system = jnp.where(grid2.strict, -mm(y, new, 1, 1), 0.0)
        d_kk = beta * d_system * within
        d_qk = d_scores * within
        d_beta = jnp.sum(y * v, axis=1, keepdims=True) + jnp.sum(d_system * t["kk"], axis=1, keepdims=True)
        flow = d_system * t["system"] + d_scores * t["scores"]
        d_cum = grid2.to_row(jnp.sum(flow, axis=1, keepdims=True)) - jnp.sum(flow, axis=0, keepdims=True)
        d_decay = jnp.sum(jnp.where(grid2.upper, d_cum, 0.0), axis=1, keepdims=True)
        d_z = d_decay * t["rate"] * jax.nn.sigmoid(t["z"])
        d_b = d_beta * beta * (1.0 - beta)
        d_ab = d_ab + jnp.where(ab_lane == h, d_z, 0.0) + jnp.where(ab_lane == heads + h, d_b, 0.0)
        d_rate = jnp.sum(d_decay * t["decay"], axis=0, keepdims=True)
        d_bias = jnp.sum(d_z, axis=0, keepdims=True)
        d_small = (
            d_small
            + jnp.where((small_row == 0) & (small_lane == h), d_rate, 0.0)
            + jnp.where((small_row == 1) & (small_lane == h), d_bias, 0.0)
        )
        d_q = mm(d_qk, k)
        d_k = mm(d_qk, q, 0, 0) + mm(d_kk, k) + mm(d_kk, k, 0, 0)
        d_v = beta * y
        d_q = unit_back(t["q_act"], t["q_norm"], d_q, dkey ** (-0.5))
        d_k = unit_back(t["k_act"], t["k_norm"], d_k, 1.0)
        for name, cot, conv_ref, cols, d_ref, d_conv_ref in (
            ("q", d_q, cq_ref, ks, dq_ref, dcq_ref),
            ("k", d_k, ck_ref, ks, dk_ref, dck_ref),
            ("v", d_v, cv_ref, vs, dv_ref, dcv_ref),
        ):
            cot = cot * silu_slope(t[name + "_pre"], t[name + "_sig"])
            d_raw, d_taps = conv_back(t[name + "_raw"], conv_ref[:, cols], cot)
            d_ref[:, cols] = d_raw.astype(bf16)
            for tap, d_tap in enumerate(d_taps):
                d_conv_ref[tap : tap + 1, cols] += d_tap
    dab_ref[...] = d_ab.astype(bf16)
    dsmall_ref[...] += d_small
    dgain_ref[...] += d_gain


def whole(shape):
    return pl.BlockSpec(shape, lambda s: (0,) * len(shape))


def by_seq(length, cols):
    return pl.BlockSpec((length, cols), lambda s: (s, 0))


def mixer_specs(length, arrays):
    q, k, v, g, ab, cq, ck, cv, rate, bias, gain = arrays
    return [by_seq(length, arr.shape[1]) for arr in (q, k, v, g, ab)] + [
        whole(arr.shape) for arr in (cq, ck, cv, rate, bias, gain)
    ]


def mixer_forward(heads, length, arrays):
    rows = arrays[0].shape[0]
    seqs = rows // length
    wide = arrays[2].shape[1]
    chunk = min(CHUNK, length)
    count = heads * (length // chunk)
    return pl.pallas_call(
        functools.partial(forward_kernel, heads),
        grid=(seqs,),
        in_specs=mixer_specs(length, arrays),
        out_specs=[
            by_seq(length, wide),
            pl.BlockSpec((1, count, chunk, chunk), lambda s: (s, 0, 0, 0)),
            by_seq(length, wide),
            by_seq(length, wide),
        ],
        out_shape=[
            jax.ShapeDtypeStruct((rows, wide), bf16),
            jax.ShapeDtypeStruct((seqs, count, chunk, chunk), f32),
            jax.ShapeDtypeStruct((rows, wide), f32),
            jax.ShapeDtypeStruct((rows, wide), f32),
        ],
        scratch_shapes=[
            pltpu.VMEM((heads, length, length), f32),
            pltpu.VMEM((heads, length, length), f32),
        ],
        compiler_params=pltpu.CompilerParams(dimension_semantics=("arbitrary",)),
        name="mixer_forward",
    )(*arrays)


def mixer_backward(heads, length, arrays, saved, d_gated):
    rows = arrays[0].shape[0]
    seqs = rows // length
    q, k, v, g, ab, cq, ck, cv, rate, bias, gain = arrays
    inv, new, out = saved
    chunk = min(CHUNK, length)
    count = heads * (length // chunk)
    small = jax.ShapeDtypeStruct((8, LANES), f32)
    raws = (q, k, v, g, ab)
    return pl.pallas_call(
        functools.partial(backward_kernel, heads),
        grid=(seqs,),
        in_specs=mixer_specs(length, arrays)
        + [pl.BlockSpec((1, count, chunk, chunk), lambda s: (s, 0, 0, 0))]
        + [by_seq(length, v.shape[1])] * 3,
        out_specs=[by_seq(length, arr.shape[1]) for arr in raws]
        + [whole(arr.shape) for arr in (cq, ck, cv, small, gain)],
        out_shape=[jax.ShapeDtypeStruct(arr.shape, bf16) for arr in raws]
        + [jax.ShapeDtypeStruct(arr.shape, f32) for arr in (cq, ck, cv, small, gain)],
        compiler_params=pltpu.CompilerParams(dimension_semantics=("arbitrary",)),
        name="mixer_backward",
    )(*arrays, inv, new, out, d_gated)


def swap(value, axis):
    size = lax.axis_size(axis)
    if size == 1:
        return jnp.zeros_like(value)
    return lax.ppermute(value, axis, [(i, i ^ 1) for i in range(size)])


def sum_over(value, axis):
    size = lax.axis_size(axis)
    if size & (size - 1):
        return lax.psum(value, axis)
    step = 1
    while step < size:
        value = value + lax.ppermute(value, axis, [(i, i ^ step) for i in range(size)])
        step *= 2
    return value


def ring_order(count):
    return list(range(0, count, 2)) + list(range(1, count, 2))[::-1]


class Ring:
    def __init__(self, axis, width):
        self.axis = axis
        size = lax.axis_size(axis)
        self.count = size // 2
        order = ring_order(self.count)
        place = [order.index(chip) for chip in range(self.count)]
        me = lax.axis_index(axis)
        core = me % 2
        pos = jnp.asarray(place, jnp.int32)[me // 2]
        self.up = [(order[p] * 2 + c, order[(p + 1) % self.count] * 2 + c) for p in range(self.count) for c in (0, 1)]
        self.down = [(dst, src) for src, dst in self.up]
        self.block = width // size
        row = lax.broadcasted_iota(jnp.int32, (self.count, self.block, width), 0)
        off = lax.broadcasted_iota(jnp.int32, (self.count, self.block, width), 1)
        col = lax.broadcasted_iota(jnp.int32, (self.count, self.block, width), 2)
        chips = jnp.asarray(order, jnp.int32)[(pos - 1 - jnp.arange(self.count)) % self.count]
        start = chips[:, None, None] * (2 * self.block) + off
        shape = (self.count * self.block, width)
        self.mine = (col == start + core * self.block).astype(bf16).reshape(shape)
        self.other = (col == start + (1 - core) * self.block).astype(bf16).reshape(shape)

    def rows(self, source):
        own = matmul_nt(self.mine, source).astype(bf16)
        sent = swap(matmul_nt(self.other, source), self.axis)
        return own, sent

    def reduce(self, partial):
        n, half = self.count, self.block // 2
        part = partial.reshape(n, 2, half, partial.shape[1])
        if n == 1:
            return partial
        going = part[0, 0]
        coming = part[n - 2, 1]
        for step in range(n - 1):
            going = lax.ppermute(going, self.axis, self.up) + part[step + 1, 0]
            coming = lax.ppermute(coming, self.axis, self.down) + part[(n - 3 - step) % n, 1]
        return jnp.concatenate([going, coming], axis=0)


def grads_kernel(row_of, starts, counts, *refs):
    pairs = max(row_of) + 1
    row_refs, refs = refs[: 2 * pairs], refs[2 * pairs :]
    own_refs, sent_refs, out_ref = refs[: len(row_of)], refs[len(row_of) : -1], refs[-1]
    step = pl.program_id(0)
    for index, pair in enumerate(row_of):

        @pl.when((step >= starts[index]) & (step < starts[index] + counts[index]))
        def _(index=index, pair=pair):
            out_ref[...] = jnp.dot(
                row_refs[2 * pair][...], own_refs[index][...], preferred_element_type=f32
            ) + jnp.dot(
                row_refs[2 * pair + 1][...].astype(bf16),
                sent_refs[index][...].astype(bf16),
                preferred_element_type=f32,
            )


def weight_grads(rows, row_of, own, sent):
    widths = [arr.shape[1] for arr in own]
    tile = math.gcd(*widths)
    counts = [width // tile for width in widths]
    starts = [sum(counts[:i]) for i in range(len(counts))]
    flat_rows = [arr for pair in rows for arr in pair]
    height, depth = flat_rows[0].shape

    def col_spec(start, count):
        return pl.BlockSpec((depth, tile), lambda j: (0, jnp.clip(j - start, 0, count - 1)))

    col_specs = [col_spec(start, count) for start, count in zip(starts, counts)]
    return pl.pallas_call(
        functools.partial(grads_kernel, tuple(row_of), tuple(starts), tuple(counts)),
        grid=(sum(counts),),
        in_specs=[pl.BlockSpec(arr.shape, lambda j: (0, 0)) for arr in flat_rows] + col_specs * 2,
        out_specs=pl.BlockSpec((height, tile), lambda j: (0, j)),
        out_shape=jax.ShapeDtypeStruct((height, sum(widths)), f32),
        compiler_params=pltpu.CompilerParams(dimension_semantics=("arbitrary",)),
        name="weight_grads",
    )(*flat_rows, *own, *sent)


def on_device(
    inputs,
    cotangent,
    lengths,
    norm1_gain,
    w_query,
    w_key,
    w_value,
    w_gate,
    w_alpha,
    w_beta,
    conv_query,
    conv_key,
    conv_value,
    a_log,
    dt_bias,
    onorm_gain,
    w_out,
    norm2_gain,
    w_one,
    w_three,
    w_two,
):
    seq_count, seq_len, width_d = inputs.shape
    row_count = seq_count * seq_len
    heads = a_log.shape[0]
    ring = Ring("dp", width_d)

    positions = lax.broadcasted_iota(jnp.int32, (seq_count, seq_len), 1)
    live_rows = (positions < lengths[:, None]).astype(f32).reshape(row_count, 1)
    x_rows = inputs.reshape(row_count, width_d).astype(f32)
    h_one = rms_scale(x_rows, norm1_gain).astype(bf16)
    w_ab = jnp.concatenate([w_alpha, w_beta], axis=1)
    matrices = (w_query, w_key, w_value, w_gate, w_ab)
    raws = tuple(
        jnp.dot(h_one, matrix, preferred_element_type=f32).astype(bf16) for matrix in matrices
    )
    arrays = raws + (
        conv_query,
        conv_key,
        conv_value,
        a_log.reshape(1, heads),
        dt_bias.reshape(1, heads),
        onorm_gain.reshape(1, -1),
    )
    gated_out, *saved = mixer_forward(heads, seq_len, arrays)
    mixed = jnp.dot(gated_out, w_out, preferred_element_type=f32)
    x_mid = x_rows + (mixed + swap(mixed, "tensor"))
    h_two = rms_scale(x_mid, norm2_gain).astype(bf16)
    pre_one = jnp.dot(h_two, w_one, preferred_element_type=f32)
    pre_three = jnp.dot(h_two, w_three, preferred_element_type=f32)
    sig_one = jax.nn.sigmoid(pre_one)
    hidden = (pre_one * sig_one * pre_three).astype(bf16)
    grad_out = cotangent.reshape(row_count, width_d).astype(f32) * live_rows
    grad_out_b = grad_out.astype(bf16)
    d_hidden = matmul_nt(grad_out_b, w_two)
    d_pre_one = (d_hidden * pre_three * sig_one * (1.0 + pre_one * (1.0 - sig_one))).astype(bf16)
    d_pre_three = (d_hidden * pre_one * sig_one).astype(bf16)
    d_h_two = matmul_nt(d_pre_one, w_one) + matmul_nt(d_pre_three, w_three)
    d_h_two = d_h_two + swap(d_h_two, "tensor")

    rows_two = ring.rows(h_two)
    rows_out = ring.rows(grad_out_b)
    ffn_cols = (d_pre_one, d_pre_three, hidden)
    ffn_sent = [swap(arr.astype(f32), "dp") for arr in ffn_cols]
    ffn_partial = weight_grads((rows_two, rows_out), (0, 0, 1), ffn_cols, ffn_sent)
    ffn_sum = ring.reduce(ffn_partial)

    ffn_out = jnp.dot(hidden, w_two, preferred_element_type=f32)
    ffn_out = ffn_out + swap(ffn_out, "tensor")
    outputs = ((x_mid + ffn_out) * live_rows).reshape(seq_count, seq_len, width_d)

    norm2_value, norm2_back = jax.vjp(rms_scale, x_mid, norm2_gain)
    d_mid_part, grad_norm2 = norm2_back(d_h_two)
    d_x_mid = grad_out + d_mid_part
    d_mid_b = d_x_mid.astype(bf16)
    d_gated = matmul_nt(d_mid_b, w_out)
    back = mixer_backward(heads, seq_len, arrays, saved, d_gated)
    d_raw, (g_conv_q, g_conv_k, g_conv_v, g_small, g_onorm) = back[:5], back[5:]

    d_h_part = matmul_nt(d_raw[0], matrices[0])
    for index_w in range(1, 5):
        d_h_part = d_h_part + matmul_nt(d_raw[index_w], matrices[index_w])
    d_h_one = d_h_part + swap(d_h_part, "tensor")
    g_onorm = g_onorm + swap(g_onorm, "tensor")
    norm1_value, norm1_back = jax.vjp(rms_scale, x_rows, norm1_gain)
    d_in_part, grad_norm1 = norm1_back(d_h_one)
    in_grad = (d_x_mid + d_in_part).reshape(seq_count, seq_len, width_d)

    rows_one = ring.rows(h_one)
    rows_mid = ring.rows(d_mid_b)
    mixer_cols = [*d_raw[:4], gated_out]
    mixer_sent = [swap(arr.astype(f32), "dp") for arr in mixer_cols]
    mixer_partial = weight_grads((rows_one, rows_mid), (0, 0, 0, 0, 1), mixer_cols, mixer_sent)
    mixer_sum = ring.reduce(mixer_partial)

    g_ab = lax.dot_general(d_raw[4], h_one, (((0,), (0,)), ((), ())), preferred_element_type=f32)
    small_parts = (grad_norm1, grad_norm2, g_conv_q, g_conv_k, g_conv_v, g_onorm, g_small, g_ab)
    sizes = [part.size // LANES for part in small_parts]
    packed = jnp.concatenate([part.reshape(-1, LANES) for part in small_parts], axis=0)
    packed = sum_over(packed, "dp")
    unpacked, offset = [], 0
    for part, size in zip(small_parts, sizes):
        unpacked.append(packed[offset : offset + size].reshape(part.shape))
        offset = offset + size
    grad_norm1, grad_norm2, g_conv_q, g_conv_k, g_conv_v, g_onorm, g_small, g_ab = unpacked
    block = width_d // lax.axis_size("dp")
    g_ab = lax.dynamic_slice_in_dim(g_ab, lax.axis_index("dp") * block, block, axis=1).T

    pieces, offset = [], 0
    for arr in mixer_cols:
        pieces.append(mixer_sum[:, offset : offset + arr.shape[1]])
        offset = offset + arr.shape[1]
    ff_local = w_one.shape[1]
    return (
        outputs,
        in_grad,
        grad_norm1,
        pieces[0],
        pieces[1],
        pieces[2],
        pieces[3],
        g_ab[:, :heads],
        g_ab[:, heads:],
        g_conv_q,
        g_conv_k,
        g_conv_v,
        g_small[0, :heads],
        g_small[1, :heads],
        g_onorm.reshape(-1),
        jnp.transpose(pieces[4]),
        grad_norm2,
        ffn_sum[:, :ff_local],
        ffn_sum[:, ff_local : 2 * ff_local],
        jnp.transpose(ffn_sum[:, 2 * ff_local :]),
    )


def solution(mesh):
    in_specs = (
        P("dp", None, None),
        P("dp", None, None),
        P("dp"),
        P(),
        P(None, "tensor"),
        P(None, "tensor"),
        P(None, "tensor"),
        P(None, "tensor"),
        P(None, "tensor"),
        P(None, "tensor"),
        P(None, "tensor"),
        P(None, "tensor"),
        P(None, "tensor"),
        P("tensor"),
        P("tensor"),
        P(),
        P("tensor", None),
        P(),
        P(None, "tensor"),
        P(None, "tensor"),
        P("tensor", None),
    )
    out_specs = (
        P("dp", None, None),
        P("dp", None, None),
        P(),
        P("dp", "tensor"),
        P("dp", "tensor"),
        P("dp", "tensor"),
        P("dp", "tensor"),
        P("dp", "tensor"),
        P("dp", "tensor"),
        P(None, "tensor"),
        P(None, "tensor"),
        P(None, "tensor"),
        P("tensor"),
        P("tensor"),
        P(),
        P("tensor", "dp"),
        P(),
        P("dp", "tensor"),
        P("dp", "tensor"),
        P("tensor", "dp"),
    )
    return jax.shard_map(
        on_device, mesh=mesh, in_specs=in_specs, out_specs=out_specs, check_vma=False
    )
```

```python
import functools
import math

import jax
import jax.numpy as jnp
from jax import lax
from jax.experimental import pallas as pl
from jax.experimental.pallas import tpu as pltpu
from jax.sharding import PartitionSpec as P


epsilon = 1e-06
DP, TENSOR = "dp", "tensor"
f32 = jnp.float32
bf16 = jnp.bfloat16
CHUNK = 128
PARTS = 2
LANES = 128


def rms_scale(rows_in, gain_in):
    return (
        rows_in * lax.rsqrt(jnp.mean(rows_in * rows_in, axis=-1, keepdims=True) + epsilon) * gain_in
    )


def matmul_nt(first_arr, second_arr):
    return lax.dot_general(
        first_arr, second_arr, (((1,), (1,)), ((), ())), preferred_element_type=f32
    )


def halves(value):
    high = value.astype(bf16)
    return high, (value - high.astype(f32)).astype(bf16)


def mm(first_arr, second_arr, first_dim=1, second_dim=0):
    first = first_arr if isinstance(first_arr, tuple) else halves(first_arr)
    second = second_arr if isinstance(second_arr, tuple) else halves(second_arr)
    dims = (((first_dim,), (second_dim,)), ((), ()))

    def one(lhs, rhs):
        return lax.dot_general(lhs, rhs, dims, preferred_element_type=f32)

    return one(first[0], second[0]) + (one(first[0], second[1]) + one(first[1], second[0]))


def delayed(series, steps):
    if steps == 0:
        return series
    rows = lax.broadcasted_iota(jnp.int32, series.shape, 0)
    return jnp.where(rows >= steps, pltpu.roll(series, steps, 0), 0.0)


def advanced(series, steps):
    if steps == 0:
        return series
    length = series.shape[0]
    rows = lax.broadcasted_iota(jnp.int32, series.shape, 0)
    return jnp.where(rows < length - steps, pltpu.roll(series, length - steps, 0), 0.0)


def conv_of(series, taps):
    count = taps.shape[0]
    total = taps[count - 1 : count] * series
    for tap in range(count - 1):
        total = total + taps[tap : tap + 1] * delayed(series, count - 1 - tap)
    return total


def conv_back(series, taps, cotangent):
    count = taps.shape[0]
    d_series = taps[count - 1 : count] * cotangent
    d_taps = []
    for tap in range(count):
        steps = count - 1 - tap
        if steps > 0:
            d_series = d_series + taps[tap : tap + 1] * advanced(cotangent, steps)
        d_taps.append(jnp.sum(cotangent * delayed(series, steps), axis=0, keepdims=True))
    return d_series, d_taps


def silu_slope(value, sig):
    return sig * (1.0 + value * (1.0 - sig))


def unit_back(act, norm, cotangent, scale):
    inner = jnp.sum(cotangent * act, axis=1, keepdims=True)
    return scale * (norm * cotangent - act * (norm * norm * norm * inner))


class Grid2:
    def __init__(self, length):
        row = lax.broadcasted_iota(jnp.int32, (length, length), 0)
        col = lax.broadcasted_iota(jnp.int32, (length, length), 1)
        self.row, self.col = row, col
        self.lower = row >= col
        self.strict = row > col
        self.upper = row <= col
        self.eye = row == col

    def to_row(self, column):
        return jnp.sum(jnp.where(self.eye, column, 0.0), axis=0, keepdims=True)


def lane_of(values, lane):
    lanes = lax.broadcasted_iota(jnp.int32, values.shape, 1)
    return jnp.sum(jnp.where(lanes == lane, values, 0.0), axis=1, keepdims=True)


class Terms:
    pass


def head_terms(raws, taps, ab, rate, bias, lane, heads, grid2):
    t = Terms()
    t.raw = raws
    t.pre = [conv_of(raw, tap) for raw, tap in zip(raws, taps)]
    t.sig = [jax.nn.sigmoid(pre) for pre in t.pre]
    t.act = [pre * sig for pre, sig in zip(t.pre, t.sig)]
    t.norm = [lax.rsqrt(jnp.sum(act * act, axis=1, keepdims=True) + epsilon) for act in t.act[:2]]
    q = t.act[0] * t.norm[0] * raws[0].shape[1] ** (-0.5)
    k = t.act[1] * t.norm[1]
    t.v = t.act[2]
    t.beta = jax.nn.sigmoid(lane_of(ab, heads + lane))
    z = lane_of(ab, lane) + lane_of(bias, lane)
    t.z = z
    t.rate = -jnp.exp(lane_of(rate, lane))
    t.decay = t.rate * (jnp.maximum(z, 0.0) + jnp.log1p(jnp.exp(-jnp.abs(z))))
    decay_row = grid2.to_row(t.decay)
    cum_col = jnp.sum(jnp.where(grid2.lower, decay_row, 0.0), axis=1, keepdims=True)
    cum_row = jnp.sum(jnp.where(grid2.upper, t.decay, 0.0), axis=0, keepdims=True)
    differ = jnp.where(grid2.lower, cum_col - cum_row, 0.0)
    t.within = jnp.where(grid2.lower, jnp.exp(differ), 0.0)
    t.q2, t.k2 = halves(q), halves(k)
    t.kk = jnp.where(grid2.strict, mm(t.k2, t.k2, 1, 1), 0.0) * t.within
    t.system = t.beta * t.kk
    t.scores = mm(t.q2, t.k2, 1, 1) * t.within
    return t


def unit_lower_inverses(blocks):
    size = blocks[0].shape[0]
    row = lax.broadcasted_iota(jnp.int32, (size, size), 0)
    col = lax.broadcasted_iota(jnp.int32, (size, size), 1)
    eye = jnp.where(row == col, 1.0, 0.0)
    half = 1
    found = None
    while half < size:
        pair = (row // (2 * half) == col // (2 * half)) & (row // half != col // half)
        parts = [jnp.where(pair, block, 0.0) for block in blocks]
        if found is None:
            found = [eye - part for part in parts]
        else:
            split = [halves(inv) for inv in found]
            left = [mm(inv, part) for inv, part in zip(split, parts)]
            found = [inv - mm(lhs, pair_inv) for inv, lhs, pair_inv in zip(found, left, split)]
        half *= 2
    return found


def forward_kernel(
    heads,
    q_ref,
    k_ref,
    v_ref,
    g_ref,
    ab_ref,
    cq_ref,
    ck_ref,
    cv_ref,
    rate_ref,
    bias_ref,
    gain_ref,
    gated_ref,
    trade_ref,
    inv_ref,
    new_ref,
    out_ref,
    system_ref,
    scores_ref,
):
    length = q_ref.shape[0]
    dv = v_ref.shape[1] // heads
    chunk = min(CHUNK, length)
    blocks = length // chunk
    grid2 = Grid2(length)
    dk = q_ref.shape[1] // heads
    ab, rate, bias = ab_ref[...].astype(f32), rate_ref[...], bias_ref[...]
    for h in range(heads):
        ks, vs = slice(h * dk, (h + 1) * dk), slice(h * dv, (h + 1) * dv)
        raws = (q_ref[:, ks].astype(f32), k_ref[:, ks].astype(f32), v_ref[:, vs].astype(f32))
        taps = (cq_ref[:, ks], ck_ref[:, ks], cv_ref[:, vs])
        t = head_terms(raws, taps, ab, rate, bias, h, heads, grid2)
        system_ref[h] = t.system
        scores_ref[h] = t.scores
        new_ref[:, h * dv : (h + 1) * dv] = t.beta * t.v
    found = unit_lower_inverses(
        [
            system_ref[h, b * chunk : (b + 1) * chunk, b * chunk : (b + 1) * chunk]
            for h in range(heads)
            for b in range(blocks)
        ]
    )
    for index, inv in enumerate(found):
        inv_ref[0, index] = inv
    for b in range(blocks):
        rows = slice(b * chunk, (b + 1) * chunk)
        for h in range(heads):
            cols = slice(h * dv, (h + 1) * dv)
            rhs = new_ref[rows, cols]
            if b > 0:
                rhs = rhs - mm(system_ref[h, rows, : b * chunk], new_ref[: b * chunk, cols])
            new_ref[rows, cols] = mm(found[h * blocks + b], rhs)
    gain = gain_ref[...]
    for h in range(heads):
        cols = slice(h * dv, (h + 1) * dv)
        out = mm(scores_ref[h], new_ref[:, cols])
        out_ref[:, cols] = out
        scaled = out * lax.rsqrt(jnp.mean(out * out, axis=1, keepdims=True) + epsilon) * gain
        gate = g_ref[:, cols].astype(f32)
        gated = (scaled * (gate * jax.nn.sigmoid(gate))).astype(bf16)
        gated_ref[:, cols] = gated
        trade_ref[:, cols] = gated.astype(f32)


def backward_kernel(first_head, heads, chained, *refs):
    (q_ref, k_ref, v_ref, g_ref, ab_ref, cq_ref, ck_ref, cv_ref, rate_ref, bias_ref, gain_ref) = refs[:11]
    (inv_ref, new_ref, out_ref, d_gated_ref, wq_ref, wk_ref, wv_ref, wg_ref, wab_ref) = refs[11:20]
    refs = refs[20:]
    dh_ref, dab_ref, dsmall_ref, dgain_ref, trade_ref, dcq_ref, dck_ref, dcv_ref = refs[-8:]
    length = q_ref.shape[0]
    dkey = q_ref.shape[1]
    chunk = min(CHUNK, length)
    blocks = length // chunk
    grid2 = Grid2(length)
    seq, head = pl.program_id(0), pl.program_id(1)
    lane = first_head + head

    for ref, index, fresh in (
        (dh_ref, 0, head == 0),
        (dab_ref, 1, head == 0),
        (dsmall_ref, 2, (head == 0) & (seq == 0)),
        (dgain_ref, 3, (head == 0) & (seq == 0)),
    ):

        @pl.when(fresh)
        def _(ref=ref, index=index):
            ref[...] = refs[index][...] if chained else jnp.zeros_like(ref)

    gain = gain_ref[...]
    raws = (q_ref[...].astype(f32), k_ref[...].astype(f32), v_ref[...].astype(f32))
    taps = (cq_ref[...], ck_ref[...], cv_ref[...])
    t = head_terms(raws, taps, ab_ref[...].astype(f32), rate_ref[...], bias_ref[...], lane, heads, grid2)
    q2, k2, v, beta, within = t.q2, t.k2, t.v, t.beta, t.within
    new2, out = halves(new_ref[...]), out_ref[...]
    d_gated = d_gated_ref[...]
    gate = g_ref[...].astype(f32)
    gate_sig = jax.nn.sigmoid(gate)
    norm = lax.rsqrt(jnp.mean(out * out, axis=1, keepdims=True) + epsilon)
    unit = out * norm
    d_gate = (d_gated * unit * gain * silu_slope(gate, gate_sig)).astype(bf16)
    d_scaled = d_gated * (gate * gate_sig)
    dgain_ref[...] += jnp.sum(d_scaled * unit, axis=0, keepdims=True)
    d_unit = d_scaled * gain
    inner = jnp.mean(d_unit * unit, axis=1, keepdims=True)
    d_out2 = halves(norm * (d_unit - unit * inner))
    d_new = mm(t.scores, d_out2, 0, 0)
    d_scores = mm(d_out2, new2, 1, 1)
    solved = [None] * blocks
    for b in reversed(range(blocks)):
        rows = slice(b * chunk, (b + 1) * chunk)
        rhs = d_new[rows]
        for later in range(b + 1, blocks):
            part = t.system[later * chunk : (later + 1) * chunk, rows]
            rhs = rhs - mm(part, solved[later], 0, 0)
        solved[b] = mm(inv_ref[0, b], rhs, 0, 0)
    y = jnp.concatenate(solved, axis=0)
    d_system = jnp.where(grid2.strict, -mm(y, new2, 1, 1), 0.0)
    d_qk2, d_kk2 = halves(d_scores * within), halves(beta * d_system * within)
    d_beta = jnp.sum(y * v, axis=1, keepdims=True) + jnp.sum(d_system * t.kk, axis=1, keepdims=True)
    flow = d_system * t.system + d_scores * t.scores
    d_cum = grid2.to_row(jnp.sum(flow, axis=1, keepdims=True)) - jnp.sum(flow, axis=0, keepdims=True)
    d_decay = jnp.sum(jnp.where(grid2.upper, d_cum, 0.0), axis=1, keepdims=True)
    d_z = d_decay * t.rate * jax.nn.sigmoid(t.z)
    d_b = d_beta * beta * (1.0 - beta)
    d_rate = jnp.sum(d_decay * t.decay, axis=0, keepdims=True)
    d_bias = jnp.sum(d_z, axis=0, keepdims=True)
    small_row = lax.broadcasted_iota(jnp.int32, dsmall_ref.shape, 0)
    small_lane = lax.broadcasted_iota(jnp.int32, dsmall_ref.shape, 1)
    dsmall_ref[...] += jnp.where((small_row == 0) & (small_lane == lane), d_rate, 0.0) + jnp.where(
        (small_row == 1) & (small_lane == lane), d_bias, 0.0
    )
    ab_lane = lax.broadcasted_iota(jnp.int32, dab_ref.shape, 1)
    d_z, d_b = d_z.astype(bf16).astype(f32), d_b.astype(bf16).astype(f32)
    dab_ref[...] += jnp.where(ab_lane == lane, d_z, 0.0) + jnp.where(ab_lane == heads + lane, d_b, 0.0)
    d_q = mm(d_qk2, k2)
    d_k = mm(d_qk2, q2, 0, 0) + mm(d_kk2, k2) + mm(d_kk2, k2, 0, 0)
    d_q = unit_back(t.act[0], t.norm[0], d_q, dkey ** (-0.5))
    d_k = unit_back(t.act[1], t.norm[1], d_k, 1.0)
    d_raws = []
    d_acts, d_conv_refs = (d_q, d_k, beta * y), (dcq_ref, dck_ref, dcv_ref)
    for cot, pre, sig, raw, tap, d_conv_ref in zip(d_acts, t.pre, t.sig, t.raw, taps, d_conv_refs):
        d_raw, d_taps = conv_back(raw, tap, cot * silu_slope(pre, sig))
        d_raws.append(d_raw.astype(bf16))
        for index, d_tap in enumerate(d_taps):
            d_conv_ref[0, index : index + 1, :] = d_tap
    d_raws.append(d_gate)
    d_h = d_z * wab_ref[pl.ds(lane, 1), :] + d_b * wab_ref[pl.ds(heads + lane, 1), :]
    start = 0
    for d_raw, w_ref in zip(d_raws, (wq_ref, wk_ref, wv_ref, wg_ref)):
        d_h = d_h + matmul_nt(d_raw, w_ref[...])
        trade_ref[:, start : start + d_raw.shape[1]] = d_raw.astype(f32)
        start += d_raw.shape[1]
    dh_ref[...] += d_h


def whole(shape):
    return pl.BlockSpec(shape, lambda s: (0,) * len(shape))


def by_seq(length, cols):
    return pl.BlockSpec((length, cols), lambda s: (s, 0))


def mixer_specs(length, arrays):
    q, k, v, g, ab, cq, ck, cv, rate, bias, gain = arrays
    return [by_seq(length, arr.shape[1]) for arr in (q, k, v, g, ab)] + [
        whole(arr.shape) for arr in (cq, ck, cv, rate, bias, gain)
    ]


def mixer_forward(heads, length, arrays):
    rows = arrays[0].shape[0]
    seqs = rows // length
    wide = arrays[2].shape[1]
    chunk = min(CHUNK, length)
    count = heads * (length // chunk)
    return pl.pallas_call(
        functools.partial(forward_kernel, heads),
        grid=(seqs,),
        in_specs=mixer_specs(length, arrays),
        out_specs=[
            by_seq(length, wide),
            by_seq(length, wide),
            pl.BlockSpec((1, count, chunk, chunk), lambda s: (s, 0, 0, 0)),
            by_seq(length, wide),
            by_seq(length, wide),
        ],
        out_shape=[
            jax.ShapeDtypeStruct((rows, wide), bf16),
            jax.ShapeDtypeStruct((rows, wide), f32),
            jax.ShapeDtypeStruct((seqs, count, chunk, chunk), f32),
            jax.ShapeDtypeStruct((rows, wide), f32),
            jax.ShapeDtypeStruct((rows, wide), f32),
        ],
        scratch_shapes=[
            pltpu.VMEM((heads, length, length), f32),
            pltpu.VMEM((heads, length, length), f32),
        ],
        name="forward",
    )(*arrays)


def mixer_backward(part, parts, heads, length, arrays, saved, d_gated, weights, before):
    rows = arrays[0].shape[0]
    seqs = rows // length
    q, _, v, _, ab, cq, ck, cv, rate, bias, gain = arrays
    inv, new, out = saved
    chunk = min(CHUNK, length)
    count = length // chunk
    own = heads // parts
    first = part * own
    width_d = weights[0].shape[0]
    dkey, dval = q.shape[1] // heads, v.shape[1] // heads
    trade = 2 * (dkey + dval)

    def seq_spec(cols):
        return pl.BlockSpec((length, cols), lambda s, h: (s, first + h))

    def col_spec(arr):
        return pl.BlockSpec((arr.shape[0], arr.shape[1] // heads), lambda s, h: (0, first + h))

    def fixed(shape):
        return pl.BlockSpec(shape, lambda s, h: (0,) * len(shape))

    def per_seq(cols):
        return pl.BlockSpec((length, cols), lambda s, h: (s, 0))

    sums = [
        (per_seq(width_d), jax.ShapeDtypeStruct((rows, width_d), f32)),
        (per_seq(ab.shape[1]), jax.ShapeDtypeStruct(ab.shape, f32)),
        (fixed((8, LANES)), jax.ShapeDtypeStruct((8, LANES), f32)),
        (fixed(gain.shape), jax.ShapeDtypeStruct(gain.shape, f32)),
    ]

    def conv_out(arr):
        cols = arr.shape[1]
        return (
            pl.BlockSpec((1, arr.shape[0], cols // heads), lambda s, h: (s, 0, h)),
            jax.ShapeDtypeStruct((seqs, arr.shape[0], cols // parts), f32),
        )

    outs = sums + [
        (
            pl.BlockSpec((length, trade), lambda s, h: (s, h)),
            jax.ShapeDtypeStruct((rows, trade * own), f32),
        )
    ]
    outs += [conv_out(arr) for arr in (cq, ck, cv)]
    before = list(before or ())
    return pl.pallas_call(
        functools.partial(backward_kernel, first, heads, bool(before)),
        grid=(seqs, own),
        in_specs=[seq_spec(dkey), seq_spec(dkey), seq_spec(dval), seq_spec(dval), per_seq(ab.shape[1])]
        + [col_spec(arr) for arr in (cq, ck, cv)]
        + [fixed(arr.shape) for arr in (rate, bias, gain)]
        + [pl.BlockSpec((1, count, chunk, chunk), lambda s, h: (s, first + h, 0, 0))]
        + [seq_spec(dval)] * 3
        + [col_spec(arr) for arr in weights[:4]]
        + [fixed(weights[4].shape)]
        + [spec for spec, _ in sums[: len(before)]],
        out_specs=[spec for spec, _ in outs],
        out_shape=[shape for _, shape in outs],
    )(*arrays, inv, new, out, d_gated, *weights, *before)


def swap(value, axis):
    size = lax.axis_size(axis)
    if size == 1:
        return jnp.zeros_like(value)
    return lax.ppermute(value, axis, [(i, i ^ 1) for i in range(size)])


def sum_over(value, axis):
    size = lax.axis_size(axis)
    if size & (size - 1):
        return lax.psum(value, axis)
    step = 1
    while step < size:
        other = lax.ppermute(value, axis, [(i, i ^ step) for i in range(size)])
        value = value + other
        step *= 2
    return value


def ring_order(count):
    return list(range(0, count, 2)) + list(range(1, count, 2))[::-1]


class Ring:
    def __init__(self, axis, width):
        self.axis = axis
        size = lax.axis_size(axis)
        self.count = size // 2
        order = ring_order(self.count)
        place = [order.index(chip) for chip in range(self.count)]
        me = lax.axis_index(axis)
        core = me % 2
        pos = jnp.asarray(place, jnp.int32)[me // 2]
        self.up = [(order[p] * 2 + c, order[(p + 1) % self.count] * 2 + c) for p in range(self.count) for c in (0, 1)]
        self.down = [(dst, src) for src, dst in self.up]
        self.block = width // size
        row = lax.broadcasted_iota(jnp.int32, (self.count, self.block, width), 0)
        off = lax.broadcasted_iota(jnp.int32, (self.count, self.block, width), 1)
        col = lax.broadcasted_iota(jnp.int32, (self.count, self.block, width), 2)
        self.firsts = sorted({0, max(self.count - 2, 0)})
        self.blocks = self.firsts + [m for m in range(self.count) if m not in self.firsts]
        turn = jnp.asarray(self.blocks, jnp.int32)
        chips = jnp.asarray(order, jnp.int32)[(pos - 1 - turn) % self.count]
        start = chips[:, None, None] * (2 * self.block) + off
        shape = (self.count * self.block, width)
        self.mine = (col == start + core * self.block).astype(bf16).reshape(shape)
        self.other = (col == start + (1 - core) * self.block).astype(bf16).reshape(shape)

    def rows(self, source):
        own = matmul_nt(self.mine, source).astype(bf16)
        sent = swap(matmul_nt(self.other, source), self.axis)
        return own, sent

    def reduce(self, partials):
        n, half = self.count, self.block // 2
        where = {}
        for arr in partials:
            for row in range(0, arr.shape[0], self.block):
                where[self.blocks[len(where)]] = (arr, row)

        def part(m, way):
            arr, row = where[m]
            return arr[row + way * half : row + (way + 1) * half]

        if n == 1:
            return partials[0]
        going, coming = part(0, 0), part(n - 2, 1)
        for step in range(n - 1):
            going = lax.ppermute(going, self.axis, self.up)
            coming = lax.ppermute(coming, self.axis, self.down)
            going = going + part(step + 1, 0)
            coming = coming + part((n - 3 - step) % n, 1)
        return jnp.concatenate([going, coming], axis=0)


def grads_kernel(row_of, starts, counts, *refs):
    pairs = max(row_of) + 1
    row_refs, refs = refs[: 2 * pairs], refs[2 * pairs :]
    own_refs, sent_refs = refs[: len(row_of)], refs[len(row_of) : -2]
    out_ref, rows_ref = refs[-2:]
    step = pl.program_id(1)
    depth = row_refs[0].shape[1]

    @pl.when(step == 0)
    def _():
        for pair in range(pairs):
            rows_ref[pair, :, :depth] = row_refs[2 * pair][...]
            rows_ref[pair, :, depth:] = row_refs[2 * pair + 1][...].astype(bf16)

    for index, pair in enumerate(row_of):

        @pl.when((step >= starts[index]) & (step < starts[index] + counts[index]))
        def _(index=index, pair=pair):
            cols = [ref[index][...].astype(bf16) for ref in (own_refs, sent_refs)]
            out_ref[...] = jnp.dot(
                rows_ref[pair], jnp.concatenate(cols, axis=0), preferred_element_type=f32
            )


def weight_grads(rows, row_of, own, sent, height, first=0, count=1):
    widths = [arr.shape[1] for arr in own]
    tile = math.gcd(*widths)
    tile = 512 if tile % 512 == 0 else tile
    counts = [width // tile for width in widths]
    starts = [sum(counts[:i]) for i in range(len(counts))]
    flat_rows = [arr for pair in rows for arr in pair]
    depth = flat_rows[0].shape[1]

    def col_spec(start, span):
        return pl.BlockSpec((depth, tile), lambda i, j: (0, jnp.clip(j - start, 0, span - 1)))

    col_specs = [col_spec(start, span) for start, span in zip(starts, counts)]
    return pl.pallas_call(
        functools.partial(grads_kernel, tuple(row_of), tuple(starts), tuple(counts)),
        grid=(count, sum(counts)),
        in_specs=[pl.BlockSpec((height, depth), lambda i, j: (first + i, 0)) for _ in flat_rows]
        + col_specs * 2,
        out_specs=pl.BlockSpec((height, tile), lambda i, j: (i, j)),
        out_shape=jax.ShapeDtypeStruct((count * height, sum(widths)), f32),
        scratch_shapes=[pltpu.VMEM((len(rows), height, 2 * depth), bf16)],
    )(*flat_rows, *own, *sent)


def layer(
    inputs,
    cotangent,
    lengths,
    norm1_gain,
    w_query,
    w_key,
    w_value,
    w_gate,
    w_alpha,
    w_beta,
    conv_query,
    conv_key,
    conv_value,
    a_log,
    dt_bias,
    onorm_gain,
    w_out,
    norm2_gain,
    w_one,
    w_three,
    w_two,
):
    seq_count, seq_len, width_d = inputs.shape
    row_count = seq_count * seq_len
    heads = a_log.shape[0]
    ring = Ring(DP, width_d)

    positions = lax.broadcasted_iota(jnp.int32, (seq_count, seq_len), 1)
    live_rows = (positions < lengths[:, None]).astype(f32).reshape(row_count, 1)
    x_rows = inputs.reshape(row_count, width_d).astype(f32)
    h_one = rms_scale(x_rows, norm1_gain).astype(bf16)
    w_ab = jnp.concatenate([w_alpha, w_beta], axis=1)
    matrices = (w_query, w_key, w_value, w_gate, w_ab)
    raws = tuple(
        jnp.dot(h_one, matrix, preferred_element_type=f32).astype(bf16) for matrix in matrices
    )
    arrays = raws + (
        conv_query,
        conv_key,
        conv_value,
        a_log.reshape(1, heads),
        dt_bias.reshape(1, heads),
        onorm_gain.reshape(1, -1),
    )
    gated_out, gated_trade, *saved = mixer_forward(heads, seq_len, arrays)
    mixed = jnp.dot(gated_out, w_out, preferred_element_type=f32)
    x_mid = x_rows + (mixed + swap(mixed, TENSOR))

    grad_out = cotangent.reshape(row_count, width_d).astype(f32) * live_rows
    grad_out_b = grad_out.astype(bf16)
    d_hidden = matmul_nt(grad_out_b, w_two)
    rows_out = ring.rows(grad_out_b)
    rows_one = ring.rows(h_one)
    gated_sent = swap(gated_trade, DP)

    h_two = rms_scale(x_mid, norm2_gain).astype(bf16)
    pre_one = jnp.dot(h_two, w_one, preferred_element_type=f32)
    pre_three = jnp.dot(h_two, w_three, preferred_element_type=f32)
    sig_one = jax.nn.sigmoid(pre_one)
    hidden = (pre_one * sig_one * pre_three).astype(bf16)
    d_pre_one = (d_hidden * pre_three * sig_one * (1.0 + pre_one * (1.0 - sig_one))).astype(bf16)
    d_pre_three = (d_hidden * pre_one * sig_one).astype(bf16)
    d_h_two = matmul_nt(d_pre_one, w_one) + matmul_nt(d_pre_three, w_three)
    d_h_two = d_h_two + swap(d_h_two, TENSOR)

    rows_two = ring.rows(h_two)
    ffn_cols = (d_pre_one, d_pre_three, hidden)
    ffn_sent = [swap(arr.astype(f32), DP) for arr in ffn_cols]
    tall = rows_two[0].shape[0]
    ffn_partial = weight_grads((rows_two, rows_out), (0, 0, 1), ffn_cols, ffn_sent, tall)
    ffn_sum = ring.reduce([ffn_partial])

    ffn_out = jnp.dot(hidden, w_two, preferred_element_type=f32)
    ffn_other = swap(ffn_out, TENSOR)

    _, norm2_back = jax.vjp(rms_scale, x_mid, norm2_gain)
    d_mid_part, grad_norm2 = norm2_back(d_h_two)
    d_x_mid = grad_out + d_mid_part
    d_mid_b = d_x_mid.astype(bf16)
    d_gated = matmul_nt(d_mid_b, w_out)
    rows_mid = ring.rows(d_mid_b)
    weights = (*matrices[:4], jnp.transpose(w_ab).astype(f32))
    sums, trades, convs = None, [], []
    for part in range(PARTS):
        back = mixer_backward(part, PARTS, heads, seq_len, arrays, saved, d_gated, weights, sums)
        sums = back[:4]
        trades.append((back[4], swap(back[4], DP)))
        convs.append([jnp.sum(conv, axis=0) for conv in back[5:]])
    d_h_part, d_ab, g_small, g_onorm = sums

    x_late, ffn_late, d_ab = lax.optimization_barrier((x_mid, ffn_out, d_ab))
    outputs = ((x_late + (ffn_late + ffn_other)) * live_rows).reshape(seq_count, seq_len, width_d)

    d_h_one = d_h_part + swap(d_h_part, TENSOR)
    g_onorm = g_onorm + swap(g_onorm, TENSOR)
    _, norm1_back = jax.vjp(rms_scale, x_rows, norm1_gain)
    d_in_part, grad_norm1 = norm1_back(d_h_one)
    in_grad = (d_x_mid + d_in_part).reshape(seq_count, seq_len, width_d)

    own = [trade[0] for trade in trades]
    sent = [trade[1] for trade in trades]
    early_rows = (0,) * (PARTS - 1) + (1,)
    grads_a = weight_grads((rows_one, rows_mid), early_rows, own[:-1] + [gated_out], sent[:-1] + [gated_sent], tall)
    grads_b = weight_grads((rows_one,), (0,), own[-1:], sent[-1:], tall)
    sum_a, sum_b = ring.reduce([grads_a]), ring.reduce([grads_b])

    g_ab = lax.dot_general(d_ab.astype(bf16), h_one, (((0,), (0,)), ((), ())), preferred_element_type=f32)
    g_convs = [conv for part in convs for conv in part]
    small_parts = (grad_norm1, grad_norm2, g_onorm, g_small, g_ab, *g_convs)
    sizes = [part.size // LANES for part in small_parts]
    packed = jnp.concatenate([part.reshape(-1, LANES) for part in small_parts], axis=0)
    packed = sum_over(packed, DP)
    unpacked, offset = [], 0
    for part, size in zip(small_parts, sizes):
        unpacked.append(packed[offset : offset + size].reshape(part.shape))
        offset = offset + size
    grad_norm1, grad_norm2, g_onorm, g_small, g_ab = unpacked[:5]
    g_conv_q, g_conv_k, g_conv_v = (jnp.concatenate(unpacked[5 + i :: 3], axis=1) for i in range(3))
    block = width_d // lax.axis_size(DP)
    g_ab = lax.dynamic_slice_in_dim(g_ab, lax.axis_index(DP) * block, block, axis=1).T

    sizes = [matrix.shape[1] // heads for matrix in matrices[:4]]
    span = sum(sizes)
    early = (heads - heads // PARTS) * span
    pieces = []
    for index, size in enumerate(sizes):
        start = sum(sizes[:index])
        cols = [sum_a[:, at + start : at + start + size] for at in range(0, early, span)]
        cols += [sum_b[:, at + start : at + start + size] for at in range(0, sum_b.shape[1], span)]
        pieces.append(jnp.concatenate(cols, axis=1))
    pieces.append(sum_a[:, early:])
    ff_local = w_one.shape[1]
    return (
        outputs,
        in_grad,
        grad_norm1,
        pieces[0],
        pieces[1],
        pieces[2],
        pieces[3],
        g_ab[:, :heads],
        g_ab[:, heads:],
        g_conv_q,
        g_conv_k,
        g_conv_v,
        g_small[0, :heads],
        g_small[1, :heads],
        g_onorm.reshape(-1),
        jnp.transpose(pieces[4]),
        grad_norm2,
        ffn_sum[:, :ff_local],
        ffn_sum[:, ff_local : 2 * ff_local],
        jnp.transpose(ffn_sum[:, 2 * ff_local :]),
    )


def solution(mesh):
    in_specs = (
        P(DP, None, None),
        P(DP, None, None),
        P(DP),
        P(),
        P(None, TENSOR),
        P(None, TENSOR),
        P(None, TENSOR),
        P(None, TENSOR),
        P(None, TENSOR),
        P(None, TENSOR),
        P(None, TENSOR),
        P(None, TENSOR),
        P(None, TENSOR),
        P(TENSOR),
        P(TENSOR),
        P(),
        P(TENSOR, None),
        P(),
        P(None, TENSOR),
        P(None, TENSOR),
        P(TENSOR, None),
    )
    out_specs = (
        P(DP, None, None),
        P(DP, None, None),
        P(),
        P(DP, TENSOR),
        P(DP, TENSOR),
        P(DP, TENSOR),
        P(DP, TENSOR),
        P(DP, TENSOR),
        P(DP, TENSOR),
        P(None, TENSOR),
        P(None, TENSOR),
        P(None, TENSOR),
        P(TENSOR),
        P(TENSOR),
        P(),
        P(TENSOR, DP),
        P(),
        P(DP, TENSOR),
        P(DP, TENSOR),
        P(TENSOR, DP),
    )
    return jax.shard_map(layer, mesh=mesh, in_specs=in_specs, out_specs=out_specs, check_vma=False)
```

```python
import functools
import math

import jax
import jax.numpy as jnp
from jax import lax
from jax.experimental import pallas as pl
from jax.experimental.pallas import tpu as pltpu
from jax.sharding import PartitionSpec as P


epsilon = 1e-06
DP, TENSOR = "dp", "tensor"
f32 = jnp.float32
bf16 = jnp.bfloat16
CHUNK = 128
PARTS = 2
LANES = 128


def rms_scale(rows_in, gain_in):
    return (
        rows_in * lax.rsqrt(jnp.mean(rows_in * rows_in, axis=-1, keepdims=True) + epsilon) * gain_in
    )


def matmul_nt(first_arr, second_arr):
    return lax.dot_general(
        first_arr, second_arr, (((1,), (1,)), ((), ())), preferred_element_type=f32
    )


def halves(value):
    high = value.astype(bf16)
    return high, (value - high.astype(f32)).astype(bf16)


def mm(first_arr, second_arr, first_dim=1, second_dim=0):
    first = first_arr if isinstance(first_arr, tuple) else halves(first_arr)
    second = second_arr if isinstance(second_arr, tuple) else halves(second_arr)
    dims = (((first_dim,), (second_dim,)), ((), ()))

    def one(lhs, rhs):
        return lax.dot_general(lhs, rhs, dims, preferred_element_type=f32)

    return one(first[0], second[0]) + (one(first[0], second[1]) + one(first[1], second[0]))


def delayed(series, steps):
    if steps == 0:
        return series
    rows = lax.broadcasted_iota(jnp.int32, series.shape, 0)
    return jnp.where(rows >= steps, pltpu.roll(series, steps, 0), 0.0)


def advanced(series, steps):
    if steps == 0:
        return series
    length = series.shape[0]
    rows = lax.broadcasted_iota(jnp.int32, series.shape, 0)
    return jnp.where(rows < length - steps, pltpu.roll(series, length - steps, 0), 0.0)


def conv_of(series, taps):
    count = taps.shape[0]
    total = taps[count - 1 : count] * series
    for tap in range(count - 1):
        total = total + taps[tap : tap + 1] * delayed(series, count - 1 - tap)
    return total


def conv_back(series, taps, cotangent):
    count = taps.shape[0]
    d_series = taps[count - 1 : count] * cotangent
    d_taps = []
    for tap in range(count):
        steps = count - 1 - tap
        if steps > 0:
            d_series = d_series + taps[tap : tap + 1] * advanced(cotangent, steps)
        d_taps.append(jnp.sum(cotangent * delayed(series, steps), axis=0, keepdims=True))
    return d_series, d_taps


def silu_slope(value, sig):
    return sig * (1.0 + value * (1.0 - sig))


def unit_back(act, norm, cotangent, scale):
    inner = jnp.sum(cotangent * act, axis=1, keepdims=True)
    return scale * (norm * cotangent - act * (norm * norm * norm * inner))


class Grid2:
    def __init__(self, length):
        row = lax.broadcasted_iota(jnp.int32, (length, length), 0)
        col = lax.broadcasted_iota(jnp.int32, (length, length), 1)
        self.row, self.col = row, col
        self.lower = row >= col
        self.strict = row > col
        self.upper = row <= col
        self.eye = row == col

    def to_row(self, column):
        return jnp.sum(jnp.where(self.eye, column, 0.0), axis=0, keepdims=True)


def lane_of(values, lane):
    lanes = lax.broadcasted_iota(jnp.int32, values.shape, 1)
    return jnp.sum(jnp.where(lanes == lane, values, 0.0), axis=1, keepdims=True)


class Terms:
    pass


def head_terms(raws, taps, ab, rate, bias, lane, heads, grid2):
    t = Terms()
    t.raw = raws
    t.pre = [conv_of(raw, tap) for raw, tap in zip(raws, taps)]
    t.sig = [jax.nn.sigmoid(pre) for pre in t.pre]
    t.act = [pre * sig for pre, sig in zip(t.pre, t.sig)]
    t.norm = [lax.rsqrt(jnp.sum(act * act, axis=1, keepdims=True) + epsilon) for act in t.act[:2]]
    q = t.act[0] * t.norm[0] * raws[0].shape[1] ** (-0.5)
    k = t.act[1] * t.norm[1]
    t.v = t.act[2]
    t.beta = jax.nn.sigmoid(lane_of(ab, heads + lane))
    z = lane_of(ab, lane) + lane_of(bias, lane)
    t.z = z
    t.rate = -jnp.exp(lane_of(rate, lane))
    t.decay = t.rate * (jnp.maximum(z, 0.0) + jnp.log1p(jnp.exp(-jnp.abs(z))))
    decay_row = grid2.to_row(t.decay)
    cum_col = jnp.sum(jnp.where(grid2.lower, decay_row, 0.0), axis=1, keepdims=True)
    cum_row = jnp.sum(jnp.where(grid2.upper, t.decay, 0.0), axis=0, keepdims=True)
    differ = jnp.where(grid2.lower, cum_col - cum_row, 0.0)
    t.within = jnp.where(grid2.lower, jnp.exp(differ), 0.0)
    t.q2, t.k2 = halves(q), halves(k)
    t.kk = jnp.where(grid2.strict, mm(t.k2, t.k2, 1, 1), 0.0) * t.within
    t.system = t.beta * t.kk
    t.scores = mm(t.q2, t.k2, 1, 1) * t.within
    return t


def unit_lower_inverses(blocks):
    size = blocks[0].shape[0]
    row = lax.broadcasted_iota(jnp.int32, (size, size), 0)
    col = lax.broadcasted_iota(jnp.int32, (size, size), 1)
    eye = jnp.where(row == col, 1.0, 0.0)
    half = 1
    found = None
    while half < size:
        pair = (row // (2 * half) == col // (2 * half)) & (row // half != col // half)
        parts = [jnp.where(pair, block, 0.0) for block in blocks]
        if found is None:
            found = [eye - part for part in parts]
        else:
            split = [halves(inv) for inv in found]
            left = [mm(inv, part) for inv, part in zip(split, parts)]
            found = [inv - mm(lhs, pair_inv) for inv, lhs, pair_inv in zip(found, left, split)]
        half *= 2
    return found


def forward_kernel(
    heads,
    q_ref,
    k_ref,
    v_ref,
    g_ref,
    ab_ref,
    cq_ref,
    ck_ref,
    cv_ref,
    rate_ref,
    bias_ref,
    gain_ref,
    gated_ref,
    trade_ref,
    inv_ref,
    new_ref,
    out_ref,
    system_ref,
    scores_ref,
):
    length = q_ref.shape[0]
    dv = v_ref.shape[1] // heads
    chunk = min(CHUNK, length)
    blocks = length // chunk
    grid2 = Grid2(length)
    dk = q_ref.shape[1] // heads
    ab, rate, bias = ab_ref[...].astype(f32), rate_ref[...], bias_ref[...]
    for h in range(heads):
        ks, vs = slice(h * dk, (h + 1) * dk), slice(h * dv, (h + 1) * dv)
        raws = (q_ref[:, ks].astype(f32), k_ref[:, ks].astype(f32), v_ref[:, vs].astype(f32))
        taps = (cq_ref[:, ks], ck_ref[:, ks], cv_ref[:, vs])
        t = head_terms(raws, taps, ab, rate, bias, h, heads, grid2)
        system_ref[h] = t.system
        scores_ref[h] = t.scores
        new_ref[:, h * dv : (h + 1) * dv] = t.beta * t.v
    found = unit_lower_inverses(
        [
            system_ref[h, b * chunk : (b + 1) * chunk, b * chunk : (b + 1) * chunk]
            for h in range(heads)
            for b in range(blocks)
        ]
    )
    for index, inv in enumerate(found):
        inv_ref[0, index] = inv
    for b in range(blocks):
        rows = slice(b * chunk, (b + 1) * chunk)
        for h in range(heads):
            cols = slice(h * dv, (h + 1) * dv)
            rhs = new_ref[rows, cols]
            if b > 0:
                rhs = rhs - mm(system_ref[h, rows, : b * chunk], new_ref[: b * chunk, cols])
            new_ref[rows, cols] = mm(found[h * blocks + b], rhs)
    gain = gain_ref[...]
    for h in range(heads):
        cols = slice(h * dv, (h + 1) * dv)
        out = mm(scores_ref[h], new_ref[:, cols])
        out_ref[:, cols] = out
        scaled = out * lax.rsqrt(jnp.mean(out * out, axis=1, keepdims=True) + epsilon) * gain
        gate = g_ref[:, cols].astype(f32)
        gated = (scaled * (gate * jax.nn.sigmoid(gate))).astype(bf16)
        gated_ref[:, cols] = gated
        trade_ref[:, cols] = gated.astype(f32)


def backward_kernel(first_head, heads, chained, *refs):
    (q_ref, k_ref, v_ref, g_ref, ab_ref, cq_ref, ck_ref, cv_ref, rate_ref, bias_ref, gain_ref) = refs[:11]
    (inv_ref, new_ref, out_ref, d_gated_ref, wq_ref, wk_ref, wv_ref, wg_ref, wab_ref) = refs[11:20]
    refs = refs[20:]
    dh_ref, dab_ref, dsmall_ref, dgain_ref, trade_ref, dcq_ref, dck_ref, dcv_ref = refs[-8:]
    length = q_ref.shape[0]
    dkey = q_ref.shape[1]
    chunk = min(CHUNK, length)
    blocks = length // chunk
    grid2 = Grid2(length)
    seq, head = pl.program_id(0), pl.program_id(1)
    lane = first_head + head

    for ref, index, fresh in (
        (dh_ref, 0, head == 0),
        (dab_ref, 1, head == 0),
        (dsmall_ref, 2, (head == 0) & (seq == 0)),
        (dgain_ref, 3, (head == 0) & (seq == 0)),
    ):

        @pl.when(fresh)
        def _(ref=ref, index=index):
            ref[...] = refs[index][...] if chained else jnp.zeros_like(ref)

    gain = gain_ref[...]
    raws = (q_ref[...].astype(f32), k_ref[...].astype(f32), v_ref[...].astype(f32))
    taps = (cq_ref[...], ck_ref[...], cv_ref[...])
    t = head_terms(raws, taps, ab_ref[...].astype(f32), rate_ref[...], bias_ref[...], lane, heads, grid2)
    q2, k2, v, beta, within = t.q2, t.k2, t.v, t.beta, t.within
    new2, out = halves(new_ref[...]), out_ref[...]
    d_gated = d_gated_ref[...]
    gate = g_ref[...].astype(f32)
    gate_sig = jax.nn.sigmoid(gate)
    norm = lax.rsqrt(jnp.mean(out * out, axis=1, keepdims=True) + epsilon)
    unit = out * norm
    d_gate = (d_gated * unit * gain * silu_slope(gate, gate_sig)).astype(bf16)
    d_scaled = d_gated * (gate * gate_sig)
    dgain_ref[...] += jnp.sum(d_scaled * unit, axis=0, keepdims=True)
    d_unit = d_scaled * gain
    inner = jnp.mean(d_unit * unit, axis=1, keepdims=True)
    d_out2 = halves(norm * (d_unit - unit * inner))
    d_new = mm(t.scores, d_out2, 0, 0)
    d_scores = mm(d_out2, new2, 1, 1)
    solved = [None] * blocks
    for b in reversed(range(blocks)):
        rows = slice(b * chunk, (b + 1) * chunk)
        rhs = d_new[rows]
        for later in range(b + 1, blocks):
            part = t.system[later * chunk : (later + 1) * chunk, rows]
            rhs = rhs - mm(part, solved[later], 0, 0)
        solved[b] = mm(inv_ref[0, b], rhs, 0, 0)
    y = jnp.concatenate(solved, axis=0)
    d_system = jnp.where(grid2.strict, -mm(y, new2, 1, 1), 0.0)
    d_qk2, d_kk2 = halves(d_scores * within), halves(beta * d_system * within)
    d_beta = jnp.sum(y * v, axis=1, keepdims=True) + jnp.sum(d_system * t.kk, axis=1, keepdims=True)
    flow = d_system * t.system + d_scores * t.scores
    d_cum = grid2.to_row(jnp.sum(flow, axis=1, keepdims=True)) - jnp.sum(flow, axis=0, keepdims=True)
    d_decay = jnp.sum(jnp.where(grid2.upper, d_cum, 0.0), axis=1, keepdims=True)
    d_z = d_decay * t.rate * jax.nn.sigmoid(t.z)
    d_b = d_beta * beta * (1.0 - beta)
    d_rate = jnp.sum(d_decay * t.decay, axis=0, keepdims=True)
    d_bias = jnp.sum(d_z, axis=0, keepdims=True)
    small_row = lax.broadcasted_iota(jnp.int32, dsmall_ref.shape, 0)
    small_lane = lax.broadcasted_iota(jnp.int32, dsmall_ref.shape, 1)
    dsmall_ref[...] += jnp.where((small_row == 0) & (small_lane == lane), d_rate, 0.0) + jnp.where(
        (small_row == 1) & (small_lane == lane), d_bias, 0.0
    )
    ab_lane = lax.broadcasted_iota(jnp.int32, dab_ref.shape, 1)
    d_z, d_b = d_z.astype(bf16).astype(f32), d_b.astype(bf16).astype(f32)
    dab_ref[...] += jnp.where(ab_lane == lane, d_z, 0.0) + jnp.where(ab_lane == heads + lane, d_b, 0.0)
    d_q = mm(d_qk2, k2)
    d_k = mm(d_qk2, q2, 0, 0) + mm(d_kk2, k2) + mm(d_kk2, k2, 0, 0)
    d_q = unit_back(t.act[0], t.norm[0], d_q, dkey ** (-0.5))
    d_k = unit_back(t.act[1], t.norm[1], d_k, 1.0)
    d_raws = []
    d_acts, d_conv_refs = (d_q, d_k, beta * y), (dcq_ref, dck_ref, dcv_ref)
    for cot, pre, sig, raw, tap, d_conv_ref in zip(d_acts, t.pre, t.sig, t.raw, taps, d_conv_refs):
        d_raw, d_taps = conv_back(raw, tap, cot * silu_slope(pre, sig))
        d_raws.append(d_raw.astype(bf16))
        for index, d_tap in enumerate(d_taps):
            d_conv_ref[0, index : index + 1, :] = d_tap
    d_raws.append(d_gate)
    d_h = d_z * wab_ref[pl.ds(lane, 1), :] + d_b * wab_ref[pl.ds(heads + lane, 1), :]
    start = 0
    for d_raw, w_ref in zip(d_raws, (wq_ref, wk_ref, wv_ref, wg_ref)):
        d_h = d_h + matmul_nt(d_raw, w_ref[...])
        trade_ref[:, start : start + d_raw.shape[1]] = d_raw.astype(f32)
        start += d_raw.shape[1]
    dh_ref[...] += d_h


def whole(shape):
    return pl.BlockSpec(shape, lambda s: (0,) * len(shape))


def by_seq(length, cols):
    return pl.BlockSpec((length, cols), lambda s: (s, 0))


def mixer_specs(length, arrays):
    q, k, v, g, ab, cq, ck, cv, rate, bias, gain = arrays
    return [by_seq(length, arr.shape[1]) for arr in (q, k, v, g, ab)] + [
        whole(arr.shape) for arr in (cq, ck, cv, rate, bias, gain)
    ]


def mixer_forward(heads, length, arrays):
    rows = arrays[0].shape[0]
    seqs = rows // length
    wide = arrays[2].shape[1]
    chunk = min(CHUNK, length)
    count = heads * (length // chunk)
    return pl.pallas_call(
        functools.partial(forward_kernel, heads),
        grid=(seqs,),
        in_specs=mixer_specs(length, arrays),
        out_specs=[
            by_seq(length, wide),
            by_seq(length, wide),
            pl.BlockSpec((1, count, chunk, chunk), lambda s: (s, 0, 0, 0)),
            by_seq(length, wide),
            by_seq(length, wide),
        ],
        out_shape=[
            jax.ShapeDtypeStruct((rows, wide), bf16),
            jax.ShapeDtypeStruct((rows, wide), f32),
            jax.ShapeDtypeStruct((seqs, count, chunk, chunk), f32),
            jax.ShapeDtypeStruct((rows, wide), f32),
            jax.ShapeDtypeStruct((rows, wide), f32),
        ],
        scratch_shapes=[
            pltpu.VMEM((heads, length, length), f32),
            pltpu.VMEM((heads, length, length), f32),
        ],
        name="forward",
    )(*arrays)


def mixer_backward(part, parts, heads, length, arrays, saved, d_gated, weights, before):
    rows = arrays[0].shape[0]
    seqs = rows // length
    q, _, v, _, ab, cq, ck, cv, rate, bias, gain = arrays
    inv, new, out = saved
    chunk = min(CHUNK, length)
    count = length // chunk
    own = heads // parts
    first = part * own
    width_d = weights[0].shape[0]
    dkey, dval = q.shape[1] // heads, v.shape[1] // heads
    trade = 2 * (dkey + dval)

    def seq_spec(cols):
        return pl.BlockSpec((length, cols), lambda s, h: (s, first + h))

    def col_spec(arr):
        return pl.BlockSpec((arr.shape[0], arr.shape[1] // heads), lambda s, h: (0, first + h))

    def fixed(shape):
        return pl.BlockSpec(shape, lambda s, h: (0,) * len(shape))

    def per_seq(cols):
        return pl.BlockSpec((length, cols), lambda s, h: (s, 0))

    sums = [
        (per_seq(width_d), jax.ShapeDtypeStruct((rows, width_d), f32)),
        (per_seq(ab.shape[1]), jax.ShapeDtypeStruct(ab.shape, f32)),
        (fixed((8, LANES)), jax.ShapeDtypeStruct((8, LANES), f32)),
        (fixed(gain.shape), jax.ShapeDtypeStruct(gain.shape, f32)),
    ]

    def conv_out(arr):
        cols = arr.shape[1]
        return (
            pl.BlockSpec((1, arr.shape[0], cols // heads), lambda s, h: (s, 0, h)),
            jax.ShapeDtypeStruct((seqs, arr.shape[0], cols // parts), f32),
        )

    outs = sums + [
        (
            pl.BlockSpec((length, trade), lambda s, h: (s, h)),
            jax.ShapeDtypeStruct((rows, trade * own), f32),
        )
    ]
    outs += [conv_out(arr) for arr in (cq, ck, cv)]
    before = list(before or ())
    return pl.pallas_call(
        functools.partial(backward_kernel, first, heads, bool(before)),
        grid=(seqs, own),
        in_specs=[seq_spec(dkey), seq_spec(dkey), seq_spec(dval), seq_spec(dval), per_seq(ab.shape[1])]
        + [col_spec(arr) for arr in (cq, ck, cv)]
        + [fixed(arr.shape) for arr in (rate, bias, gain)]
        + [pl.BlockSpec((1, count, chunk, chunk), lambda s, h: (s, first + h, 0, 0))]
        + [seq_spec(dval)] * 3
        + [col_spec(arr) for arr in weights[:4]]
        + [fixed(weights[4].shape)]
        + [spec for spec, _ in sums[: len(before)]],
        out_specs=[spec for spec, _ in outs],
        out_shape=[shape for _, shape in outs],
    )(*arrays, inv, new, out, d_gated, *weights, *before)


def swap(value, axis):
    size = lax.axis_size(axis)
    if size == 1:
        return jnp.zeros_like(value)
    return lax.ppermute(value, axis, [(i, i ^ 1) for i in range(size)])


def sum_over(value, axis):
    size = lax.axis_size(axis)
    if size & (size - 1):
        return lax.psum(value, axis)
    step = 1
    while step < size:
        other = lax.ppermute(value, axis, [(i, i ^ step) for i in range(size)])
        value = value + other
        step *= 2
    return value


def ring_order(count):
    return list(range(0, count, 2)) + list(range(1, count, 2))[::-1]


class Ring:
    def __init__(self, axis, width):
        self.axis = axis
        size = lax.axis_size(axis)
        self.count = size // 2
        order = ring_order(self.count)
        place = [order.index(chip) for chip in range(self.count)]
        me = lax.axis_index(axis)
        core = me % 2
        pos = jnp.asarray(place, jnp.int32)[me // 2]
        self.up = [(order[p] * 2 + c, order[(p + 1) % self.count] * 2 + c) for p in range(self.count) for c in (0, 1)]
        self.down = [(dst, src) for src, dst in self.up]
        self.block = width // size
        row = lax.broadcasted_iota(jnp.int32, (self.count, self.block, width), 0)
        off = lax.broadcasted_iota(jnp.int32, (self.count, self.block, width), 1)
        col = lax.broadcasted_iota(jnp.int32, (self.count, self.block, width), 2)
        self.firsts = sorted({0, max(self.count - 2, 0)})
        self.blocks = self.firsts + [m for m in range(self.count) if m not in self.firsts]
        turn = jnp.asarray(self.blocks, jnp.int32)
        chips = jnp.asarray(order, jnp.int32)[(pos - 1 - turn) % self.count]
        start = chips[:, None, None] * (2 * self.block) + off
        shape = (self.count * self.block, width)
        self.mine = (col == start + core * self.block).astype(bf16).reshape(shape)
        self.other = (col == start + (1 - core) * self.block).astype(bf16).reshape(shape)

    def rows(self, source):
        own = matmul_nt(self.mine, source).astype(bf16)
        sent = swap(matmul_nt(self.other, source), self.axis)
        return own, sent

    def reduce(self, partials):
        n, half = self.count, self.block // 2
        where = {}
        for arr in partials:
            for row in range(0, arr.shape[0], self.block):
                where[self.blocks[len(where)]] = (arr, row)

        def part(m, way):
            arr, row = where[m]
            return arr[row + way * half : row + (way + 1) * half]

        if n == 1:
            return partials[0]
        going, coming = part(0, 0), part(n - 2, 1)
        for step in range(n - 1):
            going = lax.ppermute(going, self.axis, self.up)
            coming = lax.ppermute(coming, self.axis, self.down)
            going = going + part(step + 1, 0)
            coming = coming + part((n - 3 - step) % n, 1)
        return jnp.concatenate([going, coming], axis=0)


def grads_kernel(row_of, starts, counts, *refs):
    pairs = max(row_of) + 1
    row_refs, refs = refs[: 2 * pairs], refs[2 * pairs :]
    own_refs, sent_refs = refs[: len(row_of)], refs[len(row_of) : -2]
    out_ref, rows_ref = refs[-2:]
    step = pl.program_id(0)
    depth = row_refs[0].shape[1]

    @pl.when(step == 0)
    def _():
        for pair in range(pairs):
            rows_ref[pair, :, :depth] = row_refs[2 * pair][...]
            rows_ref[pair, :, depth:] = row_refs[2 * pair + 1][...].astype(bf16)

    for index, pair in enumerate(row_of):

        @pl.when((step >= starts[index]) & (step < starts[index] + counts[index]))
        def _(index=index, pair=pair):
            cols = [ref[index][...].astype(bf16) for ref in (own_refs, sent_refs)]
            out_ref[...] = jnp.dot(
                rows_ref[pair], jnp.concatenate(cols, axis=0), preferred_element_type=f32
            )


def weight_grads(rows, cols, height):
    widths = [width for *_, width in cols]
    tile = math.gcd(*widths, *[first for *_, first, _ in cols])
    tile = 512 if tile % 512 == 0 else tile
    counts = [width // tile for width in widths]
    starts = [sum(counts[:i]) for i in range(len(counts))]
    flat_rows = [arr for pair in rows for arr in pair]
    depth = flat_rows[0].shape[1]

    def col_spec(start, span, first):
        return pl.BlockSpec((depth, tile), lambda j: (0, first + jnp.clip(j - start, 0, span - 1)))

    firsts = [first // tile for *_, first, _ in cols]
    col_specs = [col_spec(*places) for places in zip(starts, counts, firsts)]
    return pl.pallas_call(
        functools.partial(grads_kernel, tuple(pair for pair, *_ in cols), tuple(starts), tuple(counts)),
        grid=(sum(counts),),
        in_specs=[pl.BlockSpec((height, depth), lambda j: (0, 0)) for _ in flat_rows] + col_specs * 2,
        out_specs=pl.BlockSpec((height, tile), lambda j: (0, j)),
        out_shape=jax.ShapeDtypeStruct((height, sum(widths)), f32),
        scratch_shapes=[pltpu.VMEM((len(rows), height, 2 * depth), bf16)],
    )(*flat_rows, *[col[1] for col in cols], *[col[2] for col in cols])


def layer(
    inputs,
    cotangent,
    lengths,
    norm1_gain,
    w_query,
    w_key,
    w_value,
    w_gate,
    w_alpha,
    w_beta,
    conv_query,
    conv_key,
    conv_value,
    a_log,
    dt_bias,
    onorm_gain,
    w_out,
    norm2_gain,
    w_one,
    w_three,
    w_two,
):
    seq_count, seq_len, width_d = inputs.shape
    row_count = seq_count * seq_len
    heads = a_log.shape[0]
    ring = Ring(DP, width_d)

    positions = lax.broadcasted_iota(jnp.int32, (seq_count, seq_len), 1)
    live_rows = (positions < lengths[:, None]).astype(f32).reshape(row_count, 1)
    x_rows = inputs.reshape(row_count, width_d).astype(f32)
    h_one = rms_scale(x_rows, norm1_gain).astype(bf16)
    w_ab = jnp.concatenate([w_alpha, w_beta], axis=1)
    matrices = (w_query, w_key, w_value, w_gate, w_ab)
    raws = tuple(
        jnp.dot(h_one, matrix, preferred_element_type=f32).astype(bf16) for matrix in matrices
    )
    arrays = raws + (
        conv_query,
        conv_key,
        conv_value,
        a_log.reshape(1, heads),
        dt_bias.reshape(1, heads),
        onorm_gain.reshape(1, -1),
    )
    gated_out, gated_trade, *saved = mixer_forward(heads, seq_len, arrays)
    mixed = jnp.dot(gated_out, w_out, preferred_element_type=f32)
    x_mid = x_rows + (mixed + swap(mixed, TENSOR))

    grad_out = cotangent.reshape(row_count, width_d).astype(f32) * live_rows
    grad_out_b = grad_out.astype(bf16)
    d_hidden = matmul_nt(grad_out_b, w_two)
    rows_out = ring.rows(grad_out_b)
    rows_one = ring.rows(h_one)
    gated_sent = swap(gated_trade, DP)

    h_two = rms_scale(x_mid, norm2_gain).astype(bf16)
    pre_one = jnp.dot(h_two, w_one, preferred_element_type=f32)
    pre_three = jnp.dot(h_two, w_three, preferred_element_type=f32)
    sig_one = jax.nn.sigmoid(pre_one)
    hidden = (pre_one * sig_one * pre_three).astype(bf16)
    d_pre_one = (d_hidden * pre_three * sig_one * (1.0 + pre_one * (1.0 - sig_one))).astype(bf16)
    d_pre_three = (d_hidden * pre_one * sig_one).astype(bf16)
    d_h_two = matmul_nt(d_pre_one, w_one) + matmul_nt(d_pre_three, w_three)
    d_h_two = d_h_two + swap(d_h_two, TENSOR)

    rows_two = ring.rows(h_two)
    ffn_cols = (d_pre_one, d_pre_three, hidden)
    ffn_sent = [swap(arr.astype(f32), DP) for arr in ffn_cols]
    tall = rows_two[0].shape[0]
    ffn_grads = [(pair, own, sent, 0, own.shape[1]) for pair, own, sent in zip((0, 0, 1), ffn_cols, ffn_sent)]
    ffn_partial = weight_grads((rows_two, rows_out), ffn_grads, tall)
    ffn_sum = ring.reduce([ffn_partial])

    ffn_out = jnp.dot(hidden, w_two, preferred_element_type=f32)
    ffn_other = swap(ffn_out, TENSOR)

    _, norm2_back = jax.vjp(rms_scale, x_mid, norm2_gain)
    d_mid_part, grad_norm2 = norm2_back(d_h_two)
    d_x_mid = grad_out + d_mid_part
    d_mid_b = d_x_mid.astype(bf16)
    d_gated = matmul_nt(d_mid_b, w_out)
    rows_mid = ring.rows(d_mid_b)
    weights = (*matrices[:4], jnp.transpose(w_ab).astype(f32))
    sums, trades, convs = None, [], []
    for part in range(PARTS):
        back = mixer_backward(part, PARTS, heads, seq_len, arrays, saved, d_gated, weights, sums)
        sums = back[:4]
        trades.append((back[4], swap(back[4], DP)))
        convs.append([jnp.sum(conv, axis=0) for conv in back[5:]])
    d_h_part, d_ab, g_small, g_onorm = sums

    x_late, ffn_late, d_ab = lax.optimization_barrier((x_mid, ffn_out, d_ab))
    outputs = ((x_late + (ffn_late + ffn_other)) * live_rows).reshape(seq_count, seq_len, width_d)

    d_h_one = d_h_part + swap(d_h_part, TENSOR)
    g_onorm = g_onorm + swap(g_onorm, TENSOR)
    _, norm1_back = jax.vjp(rms_scale, x_rows, norm1_gain)
    d_in_part, grad_norm1 = norm1_back(d_h_one)
    in_grad = (d_x_mid + d_in_part).reshape(seq_count, seq_len, width_d)

    wide = gated_out.shape[1] // PARTS
    mixer_sums = []
    for part, (own, sent) in enumerate(trades):
        cols = [(0, own, sent, 0, own.shape[1]), (1, gated_out, gated_sent, part * wide, wide)]
        partial = weight_grads((rows_one, rows_mid), cols, tall)
        mixer_sums.append(ring.reduce([partial]))

    g_ab = lax.dot_general(d_ab.astype(bf16), h_one, (((0,), (0,)), ((), ())), preferred_element_type=f32)
    g_convs = [conv for part in convs for conv in part]
    small_parts = (grad_norm1, grad_norm2, g_onorm, g_small, g_ab, *g_convs)
    sizes = [part.size // LANES for part in small_parts]
    packed = jnp.concatenate([part.reshape(-1, LANES) for part in small_parts], axis=0)
    packed = sum_over(packed, DP)
    unpacked, offset = [], 0
    for part, size in zip(small_parts, sizes):
        unpacked.append(packed[offset : offset + size].reshape(part.shape))
        offset = offset + size
    grad_norm1, grad_norm2, g_onorm, g_small, g_ab = unpacked[:5]
    g_conv_q, g_conv_k, g_conv_v = (jnp.concatenate(unpacked[5 + i :: 3], axis=1) for i in range(3))
    block = width_d // lax.axis_size(DP)
    g_ab = lax.dynamic_slice_in_dim(g_ab, lax.axis_index(DP) * block, block, axis=1).T

    sizes = [matrix.shape[1] // heads for matrix in matrices[:4]]
    span = sum(sizes)
    heads_end = heads // PARTS * span
    pieces = []
    for index, size in enumerate(sizes):
        start = sum(sizes[:index])
        cols = [total[:, at + start : at + start + size] for total in mixer_sums for at in range(0, heads_end, span)]
        pieces.append(jnp.concatenate(cols, axis=1))
    pieces.append(jnp.concatenate([total[:, heads_end:] for total in mixer_sums], axis=1))
    ff_local = w_one.shape[1]
    return (
        outputs,
        in_grad,
        grad_norm1,
        pieces[0],
        pieces[1],
        pieces[2],
        pieces[3],
        g_ab[:, :heads],
        g_ab[:, heads:],
        g_conv_q,
        g_conv_k,
        g_conv_v,
        g_small[0, :heads],
        g_small[1, :heads],
        g_onorm.reshape(-1),
        jnp.transpose(pieces[4]),
        grad_norm2,
        ffn_sum[:, :ff_local],
        ffn_sum[:, ff_local : 2 * ff_local],
        jnp.transpose(ffn_sum[:, 2 * ff_local :]),
    )


def solution(mesh):
    in_specs = (
        P(DP, None, None),
        P(DP, None, None),
        P(DP),
        P(),
        P(None, TENSOR),
        P(None, TENSOR),
        P(None, TENSOR),
        P(None, TENSOR),
        P(None, TENSOR),
        P(None, TENSOR),
        P(None, TENSOR),
        P(None, TENSOR),
        P(None, TENSOR),
        P(TENSOR),
        P(TENSOR),
        P(),
        P(TENSOR, None),
        P(),
        P(None, TENSOR),
        P(None, TENSOR),
        P(TENSOR, None),
    )
    out_specs = (
        P(DP, None, None),
        P(DP, None, None),
        P(),
        P(DP, TENSOR),
        P(DP, TENSOR),
        P(DP, TENSOR),
        P(DP, TENSOR),
        P(DP, TENSOR),
        P(DP, TENSOR),
        P(None, TENSOR),
        P(None, TENSOR),
        P(None, TENSOR),
        P(TENSOR),
        P(TENSOR),
        P(),
        P(TENSOR, DP),
        P(),
        P(DP, TENSOR),
        P(DP, TENSOR),
        P(TENSOR, DP),
    )
    return jax.shard_map(layer, mesh=mesh, in_specs=in_specs, out_specs=out_specs, check_vma=False)
```

```python
import functools
import math

import jax
import jax.numpy as jnp
from jax import lax
from jax.experimental import pallas as pl
from jax.experimental.pallas import tpu as pltpu
from jax.sharding import PartitionSpec as P


epsilon = 1e-06
DP, TENSOR = "dp", "tensor"
f32 = jnp.float32
bf16 = jnp.bfloat16
CHUNK = 128
PARTS = 2
LANES = 128


def rms_scale(rows_in, gain_in):
    return (
        rows_in * lax.rsqrt(jnp.mean(rows_in * rows_in, axis=-1, keepdims=True) + epsilon) * gain_in
    )


def matmul_nt(first_arr, second_arr):
    return lax.dot_general(
        first_arr, second_arr, (((1,), (1,)), ((), ())), preferred_element_type=f32
    )


def halves(value):
    high = value.astype(bf16)
    return high, (value - high.astype(f32)).astype(bf16)


def mm(first_arr, second_arr, first_dim=1, second_dim=0):
    first = first_arr if isinstance(first_arr, tuple) else halves(first_arr)
    second = second_arr if isinstance(second_arr, tuple) else halves(second_arr)
    dims = (((first_dim,), (second_dim,)), ((), ()))

    def one(lhs, rhs):
        return lax.dot_general(lhs, rhs, dims, preferred_element_type=f32)

    return one(first[0], second[0]) + (one(first[0], second[1]) + one(first[1], second[0]))


def delayed(series, steps):
    if steps == 0:
        return series
    rows = lax.broadcasted_iota(jnp.int32, series.shape, 0)
    return jnp.where(rows >= steps, pltpu.roll(series, steps, 0), 0.0)


def advanced(series, steps):
    if steps == 0:
        return series
    length = series.shape[0]
    rows = lax.broadcasted_iota(jnp.int32, series.shape, 0)
    return jnp.where(rows < length - steps, pltpu.roll(series, length - steps, 0), 0.0)


def conv_of(series, taps):
    count = taps.shape[0]
    total = taps[count - 1 : count] * series
    for tap in range(count - 1):
        total = total + taps[tap : tap + 1] * delayed(series, count - 1 - tap)
    return total


def conv_back(series, taps, cotangent):
    count = taps.shape[0]
    d_series = taps[count - 1 : count] * cotangent
    d_taps = []
    for tap in range(count):
        steps = count - 1 - tap
        if steps > 0:
            d_series = d_series + taps[tap : tap + 1] * advanced(cotangent, steps)
        d_taps.append(jnp.sum(cotangent * delayed(series, steps), axis=0, keepdims=True))
    return d_series, d_taps


def silu_slope(value, sig):
    return sig * (1.0 + value * (1.0 - sig))


def unit_back(act, norm, cotangent, scale):
    inner = jnp.sum(cotangent * act, axis=1, keepdims=True)
    return scale * (norm * cotangent - act * (norm * norm * norm * inner))


class Grid2:
    def __init__(self, length):
        row = lax.broadcasted_iota(jnp.int32, (length, length), 0)
        col = lax.broadcasted_iota(jnp.int32, (length, length), 1)
        self.row, self.col = row, col
        self.lower = row >= col
        self.strict = row > col
        self.upper = row <= col
        self.eye = row == col

    def to_row(self, column):
        return jnp.sum(jnp.where(self.eye, column, 0.0), axis=0, keepdims=True)


def lane_of(values, lane):
    lanes = lax.broadcasted_iota(jnp.int32, values.shape, 1)
    return jnp.sum(jnp.where(lanes == lane, values, 0.0), axis=1, keepdims=True)


class Terms:
    pass


def head_terms(raws, taps, ab, rate, bias, lane, heads, grid2):
    t = Terms()
    t.raw = raws
    t.pre = [conv_of(raw, tap) for raw, tap in zip(raws, taps)]
    t.sig = [jax.nn.sigmoid(pre) for pre in t.pre]
    t.act = [pre * sig for pre, sig in zip(t.pre, t.sig)]
    t.norm = [lax.rsqrt(jnp.sum(act * act, axis=1, keepdims=True) + epsilon) for act in t.act[:2]]
    q = t.act[0] * t.norm[0] * raws[0].shape[1] ** (-0.5)
    k = t.act[1] * t.norm[1]
    t.v = t.act[2]
    t.beta = jax.nn.sigmoid(lane_of(ab, heads + lane))
    z = lane_of(ab, lane) + lane_of(bias, lane)
    t.z = z
    t.rate = -jnp.exp(lane_of(rate, lane))
    t.decay = t.rate * (jnp.maximum(z, 0.0) + jnp.log1p(jnp.exp(-jnp.abs(z))))
    decay_row = grid2.to_row(t.decay)
    cum_col = jnp.sum(jnp.where(grid2.lower, decay_row, 0.0), axis=1, keepdims=True)
    cum_row = jnp.sum(jnp.where(grid2.upper, t.decay, 0.0), axis=0, keepdims=True)
    differ = jnp.where(grid2.lower, cum_col - cum_row, 0.0)
    t.within = jnp.where(grid2.lower, jnp.exp(differ), 0.0)
    t.q2, t.k2 = halves(q), halves(k)
    t.kk = jnp.where(grid2.strict, mm(t.k2, t.k2, 1, 1), 0.0) * t.within
    t.system = t.beta * t.kk
    t.scores = mm(t.q2, t.k2, 1, 1) * t.within
    return t


def unit_lower_inverses(blocks_of, found_ref, count):
    size = found_ref.shape[-1]
    row = lax.broadcasted_iota(jnp.int32, (size, size), 0)
    col = lax.broadcasted_iota(jnp.int32, (size, size), 1)

    def joined(index, level):
        pair = (row >> (level + 1) == col >> (level + 1)) & (row >> level != col >> level)
        return jnp.where(pair, blocks_of(index), 0.0)

    for index in range(count):
        found_ref[0, index] = jnp.where(row == col, 1.0, 0.0) - joined(index, 0)

    def join(level, carry):
        found = [found_ref[0, index] for index in range(count)]
        split = [halves(inv) for inv in found]
        left = [mm(inv, joined(index, level)) for index, inv in enumerate(split)]
        for index in range(count):
            found_ref[0, index] = found[index] - mm(left[index], split[index])
        return carry

    lax.fori_loop(1, size.bit_length() - 1, join, 0)


def forward_kernel(
    heads,
    q_ref,
    k_ref,
    v_ref,
    g_ref,
    ab_ref,
    cq_ref,
    ck_ref,
    cv_ref,
    rate_ref,
    bias_ref,
    gain_ref,
    gated_ref,
    trade_ref,
    inv_ref,
    new_ref,
    out_ref,
    system_ref,
    scores_ref,
):
    length = q_ref.shape[0]
    dv = v_ref.shape[1] // heads
    chunk = min(CHUNK, length)
    blocks = length // chunk
    grid2 = Grid2(length)
    dk = q_ref.shape[1] // heads
    ab, rate, bias = ab_ref[...].astype(f32), rate_ref[...], bias_ref[...]

    def cols_of(h, width):
        return pl.ds(pl.multiple_of(h * width, width), width)

    def begin(h, carry):
        ks, vs = cols_of(h, dk), cols_of(h, dv)
        raws = (q_ref[:, ks].astype(f32), k_ref[:, ks].astype(f32), v_ref[:, vs].astype(f32))
        taps = (cq_ref[:, ks], ck_ref[:, ks], cv_ref[:, vs])
        t = head_terms(raws, taps, ab, rate, bias, h, heads, grid2)
        system_ref[h] = t.system
        scores_ref[h] = t.scores
        new_ref[:, vs] = t.beta * t.v
        return carry

    lax.fori_loop(0, heads, begin, 0)

    def block_of(index):
        at = slice(index % blocks * chunk, (index % blocks + 1) * chunk)
        return system_ref[index // blocks, at, at]

    unit_lower_inverses(block_of, inv_ref, heads * blocks)
    gain = gain_ref[...]

    def finish(h, carry):
        cols = cols_of(h, dv)
        for b in range(blocks):
            rows = slice(b * chunk, (b + 1) * chunk)
            rhs = new_ref[rows, cols]
            if b > 0:
                rhs = rhs - mm(system_ref[h, rows, : b * chunk], new_ref[: b * chunk, cols])
            new_ref[rows, cols] = mm(inv_ref[0, h * blocks + b], rhs)
        out = mm(scores_ref[h], new_ref[:, cols])
        out_ref[:, cols] = out
        scaled = out * lax.rsqrt(jnp.mean(out * out, axis=1, keepdims=True) + epsilon) * gain
        gate = g_ref[:, cols].astype(f32)
        gated = (scaled * (gate * jax.nn.sigmoid(gate))).astype(bf16)
        gated_ref[:, cols] = gated
        trade_ref[:, cols] = gated.astype(f32)
        return carry

    lax.fori_loop(0, heads, finish, 0)


def backward_kernel(first_head, heads, chained, *refs):
    (q_ref, k_ref, v_ref, g_ref, ab_ref, cq_ref, ck_ref, cv_ref, rate_ref, bias_ref, gain_ref) = refs[:11]
    (inv_ref, new_ref, out_ref, d_gated_ref, wq_ref, wk_ref, wv_ref, wg_ref, wab_ref) = refs[11:20]
    refs = refs[20:]
    dh_ref, dab_ref, dsmall_ref, dgain_ref, trade_ref, dcq_ref, dck_ref, dcv_ref = refs[-8:]
    length = q_ref.shape[0]
    dkey = q_ref.shape[1]
    chunk = min(CHUNK, length)
    blocks = length // chunk
    grid2 = Grid2(length)
    seq, head = pl.program_id(0), pl.program_id(1)
    lane = first_head + head

    for ref, index, fresh in (
        (dh_ref, 0, head == 0),
        (dab_ref, 1, head == 0),
        (dsmall_ref, 2, (head == 0) & (seq == 0)),
        (dgain_ref, 3, (head == 0) & (seq == 0)),
    ):

        @pl.when(fresh)
        def _(ref=ref, index=index):
            ref[...] = refs[index][...] if chained else jnp.zeros_like(ref)

    gain = gain_ref[...]
    raws = (q_ref[...].astype(f32), k_ref[...].astype(f32), v_ref[...].astype(f32))
    taps = (cq_ref[...], ck_ref[...], cv_ref[...])
    t = head_terms(raws, taps, ab_ref[...].astype(f32), rate_ref[...], bias_ref[...], lane, heads, grid2)
    q2, k2, v, beta, within = t.q2, t.k2, t.v, t.beta, t.within
    new2, out = halves(new_ref[...]), out_ref[...]
    d_gated = d_gated_ref[...]
    gate = g_ref[...].astype(f32)
    gate_sig = jax.nn.sigmoid(gate)
    norm = lax.rsqrt(jnp.mean(out * out, axis=1, keepdims=True) + epsilon)
    unit = out * norm
    d_gate = (d_gated * unit * gain * silu_slope(gate, gate_sig)).astype(bf16)
    d_scaled = d_gated * (gate * gate_sig)
    dgain_ref[...] += jnp.sum(d_scaled * unit, axis=0, keepdims=True)
    d_unit = d_scaled * gain
    inner = jnp.mean(d_unit * unit, axis=1, keepdims=True)
    d_out2 = halves(norm * (d_unit - unit * inner))
    d_new = mm(t.scores, d_out2, 0, 0)
    d_scores = mm(d_out2, new2, 1, 1)
    solved = [None] * blocks
    for b in reversed(range(blocks)):
        rows = slice(b * chunk, (b + 1) * chunk)
        rhs = d_new[rows]
        for later in range(b + 1, blocks):
            part = t.system[later * chunk : (later + 1) * chunk, rows]
            rhs = rhs - mm(part, solved[later], 0, 0)
        solved[b] = mm(inv_ref[0, b], rhs, 0, 0)
    y = jnp.concatenate(solved, axis=0)
    d_system = jnp.where(grid2.strict, -mm(y, new2, 1, 1), 0.0)
    d_qk2, d_kk2 = halves(d_scores * within), halves(beta * d_system * within)
    d_beta = jnp.sum(y * v, axis=1, keepdims=True) + jnp.sum(d_system * t.kk, axis=1, keepdims=True)
    flow = d_system * t.system + d_scores * t.scores
    d_cum = grid2.to_row(jnp.sum(flow, axis=1, keepdims=True)) - jnp.sum(flow, axis=0, keepdims=True)
    d_decay = jnp.sum(jnp.where(grid2.upper, d_cum, 0.0), axis=1, keepdims=True)
    d_z = d_decay * t.rate * jax.nn.sigmoid(t.z)
    d_b = d_beta * beta * (1.0 - beta)
    d_rate = jnp.sum(d_decay * t.decay, axis=0, keepdims=True)
    d_bias = jnp.sum(d_z, axis=0, keepdims=True)
    small_row = lax.broadcasted_iota(jnp.int32, dsmall_ref.shape, 0)
    small_lane = lax.broadcasted_iota(jnp.int32, dsmall_ref.shape, 1)
    dsmall_ref[...] += jnp.where((small_row == 0) & (small_lane == lane), d_rate, 0.0) + jnp.where(
        (small_row == 1) & (small_lane == lane), d_bias, 0.0
    )
    ab_lane = lax.broadcasted_iota(jnp.int32, dab_ref.shape, 1)
    d_z, d_b = d_z.astype(bf16).astype(f32), d_b.astype(bf16).astype(f32)
    dab_ref[...] += jnp.where(ab_lane == lane, d_z, 0.0) + jnp.where(ab_lane == heads + lane, d_b, 0.0)
    d_q = mm(d_qk2, k2)
    d_k = mm(d_qk2, q2, 0, 0) + mm(d_kk2, k2) + mm(d_kk2, k2, 0, 0)
    d_q = unit_back(t.act[0], t.norm[0], d_q, dkey ** (-0.5))
    d_k = unit_back(t.act[1], t.norm[1], d_k, 1.0)
    d_raws = []
    d_acts, d_conv_refs = (d_q, d_k, beta * y), (dcq_ref, dck_ref, dcv_ref)
    for cot, pre, sig, raw, tap, d_conv_ref in zip(d_acts, t.pre, t.sig, t.raw, taps, d_conv_refs):
        d_raw, d_taps = conv_back(raw, tap, cot * silu_slope(pre, sig))
        d_raws.append(d_raw.astype(bf16))
        for index, d_tap in enumerate(d_taps):
            d_conv_ref[0, index : index + 1, :] = d_tap
    d_raws.append(d_gate)
    d_h = d_z * wab_ref[pl.ds(lane, 1), :] + d_b * wab_ref[pl.ds(heads + lane, 1), :]
    start = 0
    for d_raw, w_ref in zip(d_raws, (wq_ref, wk_ref, wv_ref, wg_ref)):
        d_h = d_h + matmul_nt(d_raw, w_ref[...])
        trade_ref[:, start : start + d_raw.shape[1]] = d_raw.astype(f32)
        start += d_raw.shape[1]
    dh_ref[...] += d_h


def whole(shape):
    return pl.BlockSpec(shape, lambda s: (0,) * len(shape))


def by_seq(length, cols):
    return pl.BlockSpec((length, cols), lambda s: (s, 0))


def mixer_specs(length, arrays):
    q, k, v, g, ab, cq, ck, cv, rate, bias, gain = arrays
    return [by_seq(length, arr.shape[1]) for arr in (q, k, v, g, ab)] + [
        whole(arr.shape) for arr in (cq, ck, cv, rate, bias, gain)
    ]


def mixer_forward(heads, length, arrays):
    rows = arrays[0].shape[0]
    seqs = rows // length
    wide = arrays[2].shape[1]
    chunk = min(CHUNK, length)
    count = heads * (length // chunk)
    return pl.pallas_call(
        functools.partial(forward_kernel, heads),
        grid=(seqs,),
        in_specs=mixer_specs(length, arrays),
        out_specs=[
            by_seq(length, wide),
            by_seq(length, wide),
            pl.BlockSpec((1, count, chunk, chunk), lambda s: (s, 0, 0, 0)),
            by_seq(length, wide),
            by_seq(length, wide),
        ],
        out_shape=[
            jax.ShapeDtypeStruct((rows, wide), bf16),
            jax.ShapeDtypeStruct((rows, wide), f32),
            jax.ShapeDtypeStruct((seqs, count, chunk, chunk), f32),
            jax.ShapeDtypeStruct((rows, wide), f32),
            jax.ShapeDtypeStruct((rows, wide), f32),
        ],
        scratch_shapes=[
            pltpu.VMEM((heads, length, length), f32),
            pltpu.VMEM((heads, length, length), f32),
        ],
        name="forward",
    )(*arrays)


def mixer_backward(part, parts, heads, length, arrays, saved, d_gated, weights, before):
    rows = arrays[0].shape[0]
    seqs = rows // length
    q, _, v, _, ab, cq, ck, cv, rate, bias, gain = arrays
    inv, new, out = saved
    chunk = min(CHUNK, length)
    count = length // chunk
    own = heads // parts
    first = part * own
    width_d = weights[0].shape[0]
    dkey, dval = q.shape[1] // heads, v.shape[1] // heads
    trade = 2 * (dkey + dval)

    def seq_spec(cols):
        return pl.BlockSpec((length, cols), lambda s, h: (s, first + h))

    def col_spec(arr):
        return pl.BlockSpec((arr.shape[0], arr.shape[1] // heads), lambda s, h: (0, first + h))

    def fixed(shape):
        return pl.BlockSpec(shape, lambda s, h: (0,) * len(shape))

    def per_seq(cols):
        return pl.BlockSpec((length, cols), lambda s, h: (s, 0))

    sums = [
        (per_seq(width_d), jax.ShapeDtypeStruct((rows, width_d), f32)),
        (per_seq(ab.shape[1]), jax.ShapeDtypeStruct(ab.shape, f32)),
        (fixed((8, LANES)), jax.ShapeDtypeStruct((8, LANES), f32)),
        (fixed(gain.shape), jax.ShapeDtypeStruct(gain.shape, f32)),
    ]

    def conv_out(arr):
        cols = arr.shape[1]
        return (
            pl.BlockSpec((1, arr.shape[0], cols // heads), lambda s, h: (s, 0, h)),
            jax.ShapeDtypeStruct((seqs, arr.shape[0], cols // parts), f32),
        )

    outs = sums + [
        (
            pl.BlockSpec((length, trade), lambda s, h: (s, h)),
            jax.ShapeDtypeStruct((rows, trade * own), f32),
        )
    ]
    outs += [conv_out(arr) for arr in (cq, ck, cv)]
    before = list(before or ())
    return pl.pallas_call(
        functools.partial(backward_kernel, first, heads, bool(before)),
        grid=(seqs, own),
        in_specs=[seq_spec(dkey), seq_spec(dkey), seq_spec(dval), seq_spec(dval), per_seq(ab.shape[1])]
        + [col_spec(arr) for arr in (cq, ck, cv)]
        + [fixed(arr.shape) for arr in (rate, bias, gain)]
        + [pl.BlockSpec((1, count, chunk, chunk), lambda s, h: (s, first + h, 0, 0))]
        + [seq_spec(dval)] * 3
        + [col_spec(arr) for arr in weights[:4]]
        + [fixed(weights[4].shape)]
        + [spec for spec, _ in sums[: len(before)]],
        out_specs=[spec for spec, _ in outs],
        out_shape=[shape for _, shape in outs],
    )(*arrays, inv, new, out, d_gated, *weights, *before)


def swap(value, axis):
    size = lax.axis_size(axis)
    if size == 1:
        return jnp.zeros_like(value)
    return lax.ppermute(value, axis, [(i, i ^ 1) for i in range(size)])


def sum_over(value, axis):
    size = lax.axis_size(axis)
    if size & (size - 1):
        return lax.psum(value, axis)
    step = 1
    while step < size:
        other = lax.ppermute(value, axis, [(i, i ^ step) for i in range(size)])
        value = value + other
        step *= 2
    return value


def ring_order(count):
    return list(range(0, count, 2)) + list(range(1, count, 2))[::-1]


class Ring:
    def __init__(self, axis, width):
        self.axis = axis
        size = lax.axis_size(axis)
        self.count = size // 2
        order = ring_order(self.count)
        place = [order.index(chip) for chip in range(self.count)]
        me = lax.axis_index(axis)
        core = me % 2
        pos = jnp.asarray(place, jnp.int32)[me // 2]
        self.up = [(order[p] * 2 + c, order[(p + 1) % self.count] * 2 + c) for p in range(self.count) for c in (0, 1)]
        self.down = [(dst, src) for src, dst in self.up]
        self.block = width // size
        row = lax.broadcasted_iota(jnp.int32, (self.count, self.block, width), 0)
        off = lax.broadcasted_iota(jnp.int32, (self.count, self.block, width), 1)
        col = lax.broadcasted_iota(jnp.int32, (self.count, self.block, width), 2)
        self.firsts = sorted({0, max(self.count - 2, 0)})
        self.blocks = self.firsts + [m for m in range(self.count) if m not in self.firsts]
        turn = jnp.asarray(self.blocks, jnp.int32)
        chips = jnp.asarray(order, jnp.int32)[(pos - 1 - turn) % self.count]
        start = chips[:, None, None] * (2 * self.block) + off
        shape = (self.count * self.block, width)
        self.mine = (col == start + core * self.block).astype(bf16).reshape(shape)
        self.other = (col == start + (1 - core) * self.block).astype(bf16).reshape(shape)

    def rows(self, source):
        own = matmul_nt(self.mine, source).astype(bf16)
        sent = swap(matmul_nt(self.other, source), self.axis)
        return own, sent

    def reduce(self, partials):
        n, half = self.count, self.block // 2
        where = {}
        for arr in partials:
            for row in range(0, arr.shape[0], self.block):
                where[self.blocks[len(where)]] = (arr, row)

        def part(m, way):
            arr, row = where[m]
            return arr[row + way * half : row + (way + 1) * half]

        if n == 1:
            return partials[0]
        going, coming = part(0, 0), part(n - 2, 1)
        for step in range(n - 1):
            going = lax.ppermute(going, self.axis, self.up)
            coming = lax.ppermute(coming, self.axis, self.down)
            going = going + part(step + 1, 0)
            coming = coming + part((n - 3 - step) % n, 1)
        return jnp.concatenate([going, coming], axis=0)


def grads_kernel(row_of, starts, counts, *refs):
    pairs = max(row_of) + 1
    row_refs, refs = refs[: 2 * pairs], refs[2 * pairs :]
    own_refs, sent_refs = refs[: len(row_of)], refs[len(row_of) : -3]
    out_ref, rows_ref, cols_ref = refs[-3:]
    step = pl.program_id(0)
    depth = row_refs[0].shape[1]

    @pl.when(step == 0)
    def _():
        for pair in range(pairs):
            rows_ref[pair, :, :depth] = row_refs[2 * pair][...]
            rows_ref[pair, :, depth:] = row_refs[2 * pair + 1][...].astype(bf16)

    chosen = 0
    for index, pair in enumerate(row_of):
        here = (step >= starts[index]) & (step < starts[index] + counts[index])
        chosen = chosen + jnp.where(here, pair, 0)

        @pl.when(here)
        def _(index=index):
            cols_ref[:depth] = own_refs[index][...].astype(bf16)
            cols_ref[depth:] = sent_refs[index][...].astype(bf16)

    out_ref[...] = jnp.dot(rows_ref[chosen], cols_ref[...], preferred_element_type=f32)


def weight_grads(rows, cols, height):
    widths = [width for *_, width in cols]
    tile = math.gcd(*widths, *[first for *_, first, _ in cols])
    tile = 512 if tile % 512 == 0 else tile
    counts = [width // tile for width in widths]
    starts = [sum(counts[:i]) for i in range(len(counts))]
    flat_rows = [arr for pair in rows for arr in pair]
    depth = flat_rows[0].shape[1]

    def col_spec(start, span, first):
        return pl.BlockSpec((depth, tile), lambda j: (0, first + jnp.clip(j - start, 0, span - 1)))

    firsts = [first // tile for *_, first, _ in cols]
    col_specs = [col_spec(*places) for places in zip(starts, counts, firsts)]
    return pl.pallas_call(
        functools.partial(grads_kernel, tuple(pair for pair, *_ in cols), tuple(starts), tuple(counts)),
        grid=(sum(counts),),
        in_specs=[pl.BlockSpec((height, depth), lambda j: (0, 0)) for _ in flat_rows] + col_specs * 2,
        out_specs=pl.BlockSpec((height, tile), lambda j: (0, j)),
        out_shape=jax.ShapeDtypeStruct((height, sum(widths)), f32),
        scratch_shapes=[
            pltpu.VMEM((len(rows), height, 2 * depth), bf16),
            pltpu.VMEM((2 * depth, tile), bf16),
        ],
    )(*flat_rows, *[col[1] for col in cols], *[col[2] for col in cols])


def layer(
    inputs,
    cotangent,
    lengths,
    norm1_gain,
    w_query,
    w_key,
    w_value,
    w_gate,
    w_alpha,
    w_beta,
    conv_query,
    conv_key,
    conv_value,
    a_log,
    dt_bias,
    onorm_gain,
    w_out,
    norm2_gain,
    w_one,
    w_three,
    w_two,
):
    seq_count, seq_len, width_d = inputs.shape
    row_count = seq_count * seq_len
    heads = a_log.shape[0]
    ring = Ring(DP, width_d)

    positions = lax.broadcasted_iota(jnp.int32, (seq_count, seq_len), 1)
    live_rows = (positions < lengths[:, None]).astype(f32).reshape(row_count, 1)
    x_rows = inputs.reshape(row_count, width_d).astype(f32)
    h_one = rms_scale(x_rows, norm1_gain).astype(bf16)
    w_ab = jnp.concatenate([w_alpha, w_beta], axis=1)
    matrices = (w_query, w_key, w_value, w_gate, w_ab)
    raws = tuple(
        jnp.dot(h_one, matrix, preferred_element_type=f32).astype(bf16) for matrix in matrices
    )
    arrays = raws + (
        conv_query,
        conv_key,
        conv_value,
        a_log.reshape(1, heads),
        dt_bias.reshape(1, heads),
        onorm_gain.reshape(1, -1),
    )
    gated_out, gated_trade, *saved = mixer_forward(heads, seq_len, arrays)
    mixed = jnp.dot(gated_out, w_out, preferred_element_type=f32)
    x_mid = x_rows + (mixed + swap(mixed, TENSOR))

    grad_out = cotangent.reshape(row_count, width_d).astype(f32) * live_rows
    grad_out_b = grad_out.astype(bf16)
    d_hidden = matmul_nt(grad_out_b, w_two)
    rows_out = ring.rows(grad_out_b)
    rows_one = ring.rows(h_one)
    gated_sent = swap(gated_trade, DP)

    h_two = rms_scale(x_mid, norm2_gain).astype(bf16)
    pre_one = jnp.dot(h_two, w_one, preferred_element_type=f32)
    pre_three = jnp.dot(h_two, w_three, preferred_element_type=f32)
    sig_one = jax.nn.sigmoid(pre_one)
    hidden = (pre_one * sig_one * pre_three).astype(bf16)
    d_pre_one = (d_hidden * pre_three * sig_one * (1.0 + pre_one * (1.0 - sig_one))).astype(bf16)
    d_pre_three = (d_hidden * pre_one * sig_one).astype(bf16)
    d_h_two = matmul_nt(d_pre_one, w_one) + matmul_nt(d_pre_three, w_three)
    d_h_two = d_h_two + swap(d_h_two, TENSOR)

    rows_two = ring.rows(h_two)
    ffn_cols = (d_pre_one, d_pre_three, hidden)
    ffn_sent = [swap(arr.astype(f32), DP) for arr in ffn_cols]
    tall = rows_two[0].shape[0]
    ffn_grads = [(pair, own, sent, 0, own.shape[1]) for pair, own, sent in zip((0, 0, 1), ffn_cols, ffn_sent)]
    ffn_partial = weight_grads((rows_two, rows_out), ffn_grads, tall)
    ffn_sum = ring.reduce([ffn_partial])

    ffn_out = jnp.dot(hidden, w_two, preferred_element_type=f32)
    ffn_other = swap(ffn_out, TENSOR)

    _, norm2_back = jax.vjp(rms_scale, x_mid, norm2_gain)
    d_mid_part, grad_norm2 = norm2_back(d_h_two)
    d_x_mid = grad_out + d_mid_part
    d_mid_b = d_x_mid.astype(bf16)
    d_gated = matmul_nt(d_mid_b, w_out)
    rows_mid = ring.rows(d_mid_b)
    weights = (*matrices[:4], jnp.transpose(w_ab).astype(f32))
    sums, trades, convs = None, [], []
    for part in range(PARTS):
        back = mixer_backward(part, PARTS, heads, seq_len, arrays, saved, d_gated, weights, sums)
        sums = back[:4]
        trades.append((back[4], swap(back[4], DP)))
        convs.append([jnp.sum(conv, axis=0) for conv in back[5:]])
    d_h_part, d_ab, g_small, g_onorm = sums

    x_late, ffn_late, d_ab = lax.optimization_barrier((x_mid, ffn_out, d_ab))
    outputs = ((x_late + (ffn_late + ffn_other)) * live_rows).reshape(seq_count, seq_len, width_d)

    d_h_one = d_h_part + swap(d_h_part, TENSOR)
    g_onorm = g_onorm + swap(g_onorm, TENSOR)
    _, norm1_back = jax.vjp(rms_scale, x_rows, norm1_gain)
    d_in_part, grad_norm1 = norm1_back(d_h_one)
    in_grad = (d_x_mid + d_in_part).reshape(seq_count, seq_len, width_d)

    wide = gated_out.shape[1] // PARTS
    mixer_sums = []
    for part, (own, sent) in enumerate(trades):
        cols = [(0, own, sent, 0, own.shape[1]), (1, gated_out, gated_sent, part * wide, wide)]
        partial = weight_grads((rows_one, rows_mid), cols, tall)
        mixer_sums.append(ring.reduce([partial]))

    g_ab = lax.dot_general(d_ab.astype(bf16), h_one, (((0,), (0,)), ((), ())), preferred_element_type=f32)
    g_convs = [conv for part in convs for conv in part]
    small_parts = (grad_norm1, grad_norm2, g_onorm, g_small, g_ab, *g_convs)
    sizes = [part.size // LANES for part in small_parts]
    packed = jnp.concatenate([part.reshape(-1, LANES) for part in small_parts], axis=0)
    packed = sum_over(packed, DP)
    unpacked, offset = [], 0
    for part, size in zip(small_parts, sizes):
        unpacked.append(packed[offset : offset + size].reshape(part.shape))
        offset = offset + size
    grad_norm1, grad_norm2, g_onorm, g_small, g_ab = unpacked[:5]
    g_conv_q, g_conv_k, g_conv_v = (jnp.concatenate(unpacked[5 + i :: 3], axis=1) for i in range(3))
    block = width_d // lax.axis_size(DP)
    g_ab = lax.dynamic_slice_in_dim(g_ab, lax.axis_index(DP) * block, block, axis=1).T

    sizes = [matrix.shape[1] // heads for matrix in matrices[:4]]
    span = sum(sizes)
    heads_end = heads // PARTS * span
    pieces = []
    for index, size in enumerate(sizes):
        start = sum(sizes[:index])
        cols = [total[:, at + start : at + start + size] for total in mixer_sums for at in range(0, heads_end, span)]
        pieces.append(jnp.concatenate(cols, axis=1))
    pieces.append(jnp.concatenate([total[:, heads_end:] for total in mixer_sums], axis=1))
    ff_local = w_one.shape[1]
    return (
        outputs,
        in_grad,
        grad_norm1,
        pieces[0],
        pieces[1],
        pieces[2],
        pieces[3],
        g_ab[:, :heads],
        g_ab[:, heads:],
        g_conv_q,
        g_conv_k,
        g_conv_v,
        g_small[0, :heads],
        g_small[1, :heads],
        g_onorm.reshape(-1),
        jnp.transpose(pieces[4]),
        grad_norm2,
        ffn_sum[:, :ff_local],
        ffn_sum[:, ff_local : 2 * ff_local],
        jnp.transpose(ffn_sum[:, 2 * ff_local :]),
    )


def solution(mesh):
    in_specs = (
        P(DP, None, None),
        P(DP, None, None),
        P(DP),
        P(),
        P(None, TENSOR),
        P(None, TENSOR),
        P(None, TENSOR),
        P(None, TENSOR),
        P(None, TENSOR),
        P(None, TENSOR),
        P(None, TENSOR),
        P(None, TENSOR),
        P(None, TENSOR),
        P(TENSOR),
        P(TENSOR),
        P(),
        P(TENSOR, None),
        P(),
        P(None, TENSOR),
        P(None, TENSOR),
        P(TENSOR, None),
    )
    out_specs = (
        P(DP, None, None),
        P(DP, None, None),
        P(),
        P(DP, TENSOR),
        P(DP, TENSOR),
        P(DP, TENSOR),
        P(DP, TENSOR),
        P(DP, TENSOR),
        P(DP, TENSOR),
        P(None, TENSOR),
        P(None, TENSOR),
        P(None, TENSOR),
        P(TENSOR),
        P(TENSOR),
        P(),
        P(TENSOR, DP),
        P(),
        P(DP, TENSOR),
        P(DP, TENSOR),
        P(TENSOR, DP),
    )
    return jax.shard_map(layer, mesh=mesh, in_specs=in_specs, out_specs=out_specs, check_vma=False)
```

```python
import functools
import math

import jax
import jax.numpy as jnp
from jax import lax
from jax.experimental import pallas as pl
from jax.experimental.pallas import tpu as pltpu
from jax.sharding import PartitionSpec as P


epsilon = 1e-06
DP, TENSOR = "dp", "tensor"
f32 = jnp.float32
bf16 = jnp.bfloat16
CHUNK = 128
PARTS = 2
LANES = 128


def rms_scale(rows_in, gain_in):
    return (
        rows_in * lax.rsqrt(jnp.mean(rows_in * rows_in, axis=-1, keepdims=True) + epsilon) * gain_in
    )


def matmul_nt(first_arr, second_arr):
    return lax.dot_general(
        first_arr, second_arr, (((1,), (1,)), ((), ())), preferred_element_type=f32
    )


def halves(value):
    high = value.astype(bf16)
    return high, (value - high.astype(f32)).astype(bf16)


def mm(first_arr, second_arr, first_dim=1, second_dim=0):
    first = first_arr if isinstance(first_arr, tuple) else halves(first_arr)
    second = second_arr if isinstance(second_arr, tuple) else halves(second_arr)
    dims = (((first_dim,), (second_dim,)), ((), ()))

    def one(lhs, rhs):
        return lax.dot_general(lhs, rhs, dims, preferred_element_type=f32)

    return one(first[0], second[0]) + (one(first[0], second[1]) + one(first[1], second[0]))


def delayed(series, steps):
    if steps == 0:
        return series
    rows = lax.broadcasted_iota(jnp.int32, series.shape, 0)
    return jnp.where(rows >= steps, pltpu.roll(series, steps, 0), 0.0)


def advanced(series, steps):
    if steps == 0:
        return series
    length = series.shape[0]
    rows = lax.broadcasted_iota(jnp.int32, series.shape, 0)
    return jnp.where(rows < length - steps, pltpu.roll(series, length - steps, 0), 0.0)


def conv_of(series, taps):
    count = taps.shape[0]
    total = taps[count - 1 : count] * series
    for tap in range(count - 1):
        total = total + taps[tap : tap + 1] * delayed(series, count - 1 - tap)
    return total


def conv_back(series, taps, cotangent):
    count = taps.shape[0]
    d_series = taps[count - 1 : count] * cotangent
    d_taps = []
    for tap in range(count):
        steps = count - 1 - tap
        if steps > 0:
            d_series = d_series + taps[tap : tap + 1] * advanced(cotangent, steps)
        d_taps.append(jnp.sum(cotangent * delayed(series, steps), axis=0, keepdims=True))
    return d_series, d_taps


def silu_slope(value, sig):
    return sig * (1.0 + value * (1.0 - sig))


def unit_back(act, norm, cotangent, scale):
    inner = jnp.sum(cotangent * act, axis=1, keepdims=True)
    return scale * (norm * cotangent - act * (norm * norm * norm * inner))


class Grid2:
    def __init__(self, length):
        row = lax.broadcasted_iota(jnp.int32, (length, length), 0)
        col = lax.broadcasted_iota(jnp.int32, (length, length), 1)
        self.row, self.col = row, col
        self.lower = row >= col
        self.strict = row > col
        self.upper = row <= col
        self.eye = row == col

    def to_row(self, column):
        return jnp.sum(jnp.where(self.eye, column, 0.0), axis=0, keepdims=True)


def lane_of(values, lane):
    lanes = lax.broadcasted_iota(jnp.int32, values.shape, 1)
    return jnp.sum(jnp.where(lanes == lane, values, 0.0), axis=1, keepdims=True)


class Terms:
    pass


def head_terms(raws, taps, ab, rate, bias, lane, heads, grid2):
    t = Terms()
    t.raw = raws
    t.pre = [conv_of(raw, tap) for raw, tap in zip(raws, taps)]
    t.sig = [jax.nn.sigmoid(pre) for pre in t.pre]
    t.act = [pre * sig for pre, sig in zip(t.pre, t.sig)]
    t.norm = [lax.rsqrt(jnp.sum(act * act, axis=1, keepdims=True) + epsilon) for act in t.act[:2]]
    q = t.act[0] * t.norm[0] * raws[0].shape[1] ** (-0.5)
    k = t.act[1] * t.norm[1]
    t.v = t.act[2]
    t.beta = jax.nn.sigmoid(lane_of(ab, heads + lane))
    z = lane_of(ab, lane) + lane_of(bias, lane)
    t.z = z
    t.rate = -jnp.exp(lane_of(rate, lane))
    t.decay = t.rate * (jnp.maximum(z, 0.0) + jnp.log1p(jnp.exp(-jnp.abs(z))))
    decay_row = grid2.to_row(t.decay)
    cum_col = jnp.sum(jnp.where(grid2.lower, decay_row, 0.0), axis=1, keepdims=True)
    cum_row = jnp.sum(jnp.where(grid2.upper, t.decay, 0.0), axis=0, keepdims=True)
    differ = jnp.where(grid2.lower, cum_col - cum_row, 0.0)
    t.within = jnp.where(grid2.lower, jnp.exp(differ), 0.0)
    t.q2, t.k2 = halves(q), halves(k)
    t.kk = jnp.where(grid2.strict, mm(t.k2, t.k2, 1, 1), 0.0) * t.within
    t.system = t.beta * t.kk
    t.scores = mm(t.q2, t.k2, 1, 1) * t.within
    return t


def unit_lower_inverses(blocks_of, found_ref, count):
    size = found_ref.shape[-1]
    row = lax.broadcasted_iota(jnp.int32, (size, size), 0)
    col = lax.broadcasted_iota(jnp.int32, (size, size), 1)

    def joined(index, level):
        pair = (row >> (level + 1) == col >> (level + 1)) & (row >> level != col >> level)
        return jnp.where(pair, blocks_of(index), 0.0)

    for index in range(count):
        found_ref[0, index] = jnp.where(row == col, 1.0, 0.0) - joined(index, 0)

    def join(level, carry):
        found = [found_ref[0, index] for index in range(count)]
        split = [halves(inv) for inv in found]
        left = [mm(inv, joined(index, level)) for index, inv in enumerate(split)]
        for index in range(count):
            found_ref[0, index] = found[index] - mm(left[index], split[index])
        return carry

    lax.fori_loop(1, size.bit_length() - 1, join, 0)


def forward_kernel(
    heads,
    q_ref,
    k_ref,
    v_ref,
    g_ref,
    ab_ref,
    cq_ref,
    ck_ref,
    cv_ref,
    rate_ref,
    bias_ref,
    gain_ref,
    gated_ref,
    trade_ref,
    inv_ref,
    new_ref,
    out_ref,
    system_ref,
    scores_ref,
):
    length = q_ref.shape[0]
    dv = v_ref.shape[1] // heads
    chunk = min(CHUNK, length)
    blocks = length // chunk
    grid2 = Grid2(length)
    dk = q_ref.shape[1] // heads
    ab, rate, bias = ab_ref[...].astype(f32), rate_ref[...], bias_ref[...]

    def cols_of(h, width):
        return pl.ds(pl.multiple_of(h * width, width), width)

    def begin(h, carry):
        ks, vs = cols_of(h, dk), cols_of(h, dv)
        raws = (q_ref[:, ks].astype(f32), k_ref[:, ks].astype(f32), v_ref[:, vs].astype(f32))
        taps = (cq_ref[:, ks], ck_ref[:, ks], cv_ref[:, vs])
        t = head_terms(raws, taps, ab, rate, bias, h, heads, grid2)
        system_ref[h] = t.system
        scores_ref[h] = t.scores
        new_ref[:, vs] = t.beta * t.v
        return carry

    lax.fori_loop(0, heads, begin, 0, unroll=2)

    def block_of(index):
        at = slice(index % blocks * chunk, (index % blocks + 1) * chunk)
        return system_ref[index // blocks, at, at]

    unit_lower_inverses(block_of, inv_ref, heads * blocks)
    gain = gain_ref[...]

    def finish(h, carry):
        cols = cols_of(h, dv)
        for b in range(blocks):
            rows = slice(b * chunk, (b + 1) * chunk)
            rhs = new_ref[rows, cols]
            if b > 0:
                rhs = rhs - mm(system_ref[h, rows, : b * chunk], new_ref[: b * chunk, cols])
            new_ref[rows, cols] = mm(inv_ref[0, h * blocks + b], rhs)
        out = mm(scores_ref[h], new_ref[:, cols])
        out_ref[:, cols] = out
        scaled = out * lax.rsqrt(jnp.mean(out * out, axis=1, keepdims=True) + epsilon) * gain
        gate = g_ref[:, cols].astype(f32)
        gated = (scaled * (gate * jax.nn.sigmoid(gate))).astype(bf16)
        gated_ref[:, cols] = gated
        trade_ref[:, cols] = gated.astype(f32)
        return carry

    lax.fori_loop(0, heads, finish, 0)


def backward_kernel(first_head, heads, chained, *refs):
    (q_ref, k_ref, v_ref, g_ref, ab_ref, cq_ref, ck_ref, cv_ref, rate_ref, bias_ref, gain_ref) = refs[:11]
    (inv_ref, new_ref, out_ref, d_gated_ref, wq_ref, wk_ref, wv_ref, wg_ref, wab_ref) = refs[11:20]
    refs = refs[20:]
    dh_ref, dab_ref, dsmall_ref, dgain_ref, trade_ref, dcq_ref, dck_ref, dcv_ref = refs[-8:]
    length = q_ref.shape[0]
    dkey = q_ref.shape[1]
    chunk = min(CHUNK, length)
    blocks = length // chunk
    grid2 = Grid2(length)
    seq, head = pl.program_id(0), pl.program_id(1)
    lane = first_head + head

    for ref, index, fresh in (
        (dh_ref, 0, head == 0),
        (dab_ref, 1, head == 0),
        (dsmall_ref, 2, (head == 0) & (seq == 0)),
        (dgain_ref, 3, (head == 0) & (seq == 0)),
    ):

        @pl.when(fresh)
        def _(ref=ref, index=index):
            ref[...] = refs[index][...] if chained else jnp.zeros_like(ref)

    gain = gain_ref[...]
    raws = (q_ref[...].astype(f32), k_ref[...].astype(f32), v_ref[...].astype(f32))
    taps = (cq_ref[...], ck_ref[...], cv_ref[...])
    t = head_terms(raws, taps, ab_ref[...].astype(f32), rate_ref[...], bias_ref[...], lane, heads, grid2)
    q2, k2, v, beta, within = t.q2, t.k2, t.v, t.beta, t.within
    new2, out = halves(new_ref[...]), out_ref[...]
    d_gated = d_gated_ref[...]
    gate = g_ref[...].astype(f32)
    gate_sig = jax.nn.sigmoid(gate)
    norm = lax.rsqrt(jnp.mean(out * out, axis=1, keepdims=True) + epsilon)
    unit = out * norm
    d_gate = (d_gated * unit * gain * silu_slope(gate, gate_sig)).astype(bf16)
    d_scaled = d_gated * (gate * gate_sig)
    dgain_ref[...] += jnp.sum(d_scaled * unit, axis=0, keepdims=True)
    d_unit = d_scaled * gain
    inner = jnp.mean(d_unit * unit, axis=1, keepdims=True)
    d_out2 = halves(norm * (d_unit - unit * inner))
    d_new = mm(t.scores, d_out2, 0, 0)
    d_scores = mm(d_out2, new2, 1, 1)
    solved = [None] * blocks
    for b in reversed(range(blocks)):
        rows = slice(b * chunk, (b + 1) * chunk)
        rhs = d_new[rows]
        for later in range(b + 1, blocks):
            part = t.system[later * chunk : (later + 1) * chunk, rows]
            rhs = rhs - mm(part, solved[later], 0, 0)
        solved[b] = mm(inv_ref[0, b], rhs, 0, 0)
    y = jnp.concatenate(solved, axis=0)
    d_system = jnp.where(grid2.strict, -mm(y, new2, 1, 1), 0.0)
    d_qk2, d_kk2 = halves(d_scores * within), halves(beta * d_system * within)
    d_beta = jnp.sum(y * v, axis=1, keepdims=True) + jnp.sum(d_system * t.kk, axis=1, keepdims=True)
    flow = d_system * t.system + d_scores * t.scores
    d_cum = grid2.to_row(jnp.sum(flow, axis=1, keepdims=True)) - jnp.sum(flow, axis=0, keepdims=True)
    d_decay = jnp.sum(jnp.where(grid2.upper, d_cum, 0.0), axis=1, keepdims=True)
    d_z = d_decay * t.rate * jax.nn.sigmoid(t.z)
    d_b = d_beta * beta * (1.0 - beta)
    d_rate = jnp.sum(d_decay * t.decay, axis=0, keepdims=True)
    d_bias = jnp.sum(d_z, axis=0, keepdims=True)
    small_row = lax.broadcasted_iota(jnp.int32, dsmall_ref.shape, 0)
    small_lane = lax.broadcasted_iota(jnp.int32, dsmall_ref.shape, 1)
    dsmall_ref[...] += jnp.where((small_row == 0) & (small_lane == lane), d_rate, 0.0) + jnp.where(
        (small_row == 1) & (small_lane == lane), d_bias, 0.0
    )
    ab_lane = lax.broadcasted_iota(jnp.int32, dab_ref.shape, 1)
    d_z, d_b = d_z.astype(bf16).astype(f32), d_b.astype(bf16).astype(f32)
    dab_ref[...] += jnp.where(ab_lane == lane, d_z, 0.0) + jnp.where(ab_lane == heads + lane, d_b, 0.0)
    d_q = mm(d_qk2, k2)
    d_k = mm(d_qk2, q2, 0, 0) + mm(d_kk2, k2) + mm(d_kk2, k2, 0, 0)
    d_q = unit_back(t.act[0], t.norm[0], d_q, dkey ** (-0.5))
    d_k = unit_back(t.act[1], t.norm[1], d_k, 1.0)
    d_raws = []
    d_acts, d_conv_refs = (d_q, d_k, beta * y), (dcq_ref, dck_ref, dcv_ref)
    for cot, pre, sig, raw, tap, d_conv_ref in zip(d_acts, t.pre, t.sig, t.raw, taps, d_conv_refs):
        d_raw, d_taps = conv_back(raw, tap, cot * silu_slope(pre, sig))
        d_raws.append(d_raw.astype(bf16))
        for index, d_tap in enumerate(d_taps):
            d_conv_ref[0, index : index + 1, :] = d_tap
    d_raws.append(d_gate)
    d_h = d_z * wab_ref[pl.ds(lane, 1), :] + d_b * wab_ref[pl.ds(heads + lane, 1), :]
    start = 0
    for d_raw, w_ref in zip(d_raws, (wq_ref, wk_ref, wv_ref, wg_ref)):
        d_h = d_h + matmul_nt(d_raw, w_ref[...])
        trade_ref[:, start : start + d_raw.shape[1]] = d_raw.astype(f32)
        start += d_raw.shape[1]
    dh_ref[...] += d_h


def whole(shape):
    return pl.BlockSpec(shape, lambda s: (0,) * len(shape))


def by_seq(length, cols):
    return pl.BlockSpec((length, cols), lambda s: (s, 0))


def mixer_specs(length, arrays):
    q, k, v, g, ab, cq, ck, cv, rate, bias, gain = arrays
    return [by_seq(length, arr.shape[1]) for arr in (q, k, v, g, ab)] + [
        whole(arr.shape) for arr in (cq, ck, cv, rate, bias, gain)
    ]


def mixer_forward(heads, length, arrays):
    rows = arrays[0].shape[0]
    seqs = rows // length
    wide = arrays[2].shape[1]
    chunk = min(CHUNK, length)
    count = heads * (length // chunk)
    return pl.pallas_call(
        functools.partial(forward_kernel, heads),
        grid=(seqs,),
        in_specs=mixer_specs(length, arrays),
        out_specs=[
            by_seq(length, wide),
            by_seq(length, wide),
            pl.BlockSpec((1, count, chunk, chunk), lambda s: (s, 0, 0, 0)),
            by_seq(length, wide),
            by_seq(length, wide),
        ],
        out_shape=[
            jax.ShapeDtypeStruct((rows, wide), bf16),
            jax.ShapeDtypeStruct((rows, wide), f32),
            jax.ShapeDtypeStruct((seqs, count, chunk, chunk), f32),
            jax.ShapeDtypeStruct((rows, wide), f32),
            jax.ShapeDtypeStruct((rows, wide), f32),
        ],
        scratch_shapes=[
            pltpu.VMEM((heads, length, length), f32),
            pltpu.VMEM((heads, length, length), f32),
        ],
        name="forward",
    )(*arrays)


def mixer_backward(part, parts, heads, length, arrays, saved, d_gated, weights, before):
    rows = arrays[0].shape[0]
    seqs = rows // length
    q, _, v, _, ab, cq, ck, cv, rate, bias, gain = arrays
    inv, new, out = saved
    chunk = min(CHUNK, length)
    count = length // chunk
    own = heads // parts
    first = part * own
    width_d = weights[0].shape[0]
    dkey, dval = q.shape[1] // heads, v.shape[1] // heads
    trade = 2 * (dkey + dval)

    def seq_spec(cols):
        return pl.BlockSpec((length, cols), lambda s, h: (s, first + h))

    def col_spec(arr):
        return pl.BlockSpec((arr.shape[0], arr.shape[1] // heads), lambda s, h: (0, first + h))

    def fixed(shape):
        return pl.BlockSpec(shape, lambda s, h: (0,) * len(shape))

    def per_seq(cols):
        return pl.BlockSpec((length, cols), lambda s, h: (s, 0))

    sums = [
        (per_seq(width_d), jax.ShapeDtypeStruct((rows, width_d), f32)),
        (per_seq(ab.shape[1]), jax.ShapeDtypeStruct(ab.shape, f32)),
        (fixed((8, LANES)), jax.ShapeDtypeStruct((8, LANES), f32)),
        (fixed(gain.shape), jax.ShapeDtypeStruct(gain.shape, f32)),
    ]

    def conv_out(arr):
        cols = arr.shape[1]
        return (
            pl.BlockSpec((1, arr.shape[0], cols // heads), lambda s, h: (s, 0, h)),
            jax.ShapeDtypeStruct((seqs, arr.shape[0], cols // parts), f32),
        )

    outs = sums + [
        (
            pl.BlockSpec((length, trade), lambda s, h: (s, h)),
            jax.ShapeDtypeStruct((rows, trade * own), f32),
        )
    ]
    outs += [conv_out(arr) for arr in (cq, ck, cv)]
    before = list(before or ())
    return pl.pallas_call(
        functools.partial(backward_kernel, first, heads, bool(before)),
        grid=(seqs, own),
        in_specs=[seq_spec(dkey), seq_spec(dkey), seq_spec(dval), seq_spec(dval), per_seq(ab.shape[1])]
        + [col_spec(arr) for arr in (cq, ck, cv)]
        + [fixed(arr.shape) for arr in (rate, bias, gain)]
        + [pl.BlockSpec((1, count, chunk, chunk), lambda s, h: (s, first + h, 0, 0))]
        + [seq_spec(dval)] * 3
        + [col_spec(arr) for arr in weights[:4]]
        + [fixed(weights[4].shape)]
        + [spec for spec, _ in sums[: len(before)]],
        out_specs=[spec for spec, _ in outs],
        out_shape=[shape for _, shape in outs],
    )(*arrays, inv, new, out, d_gated, *weights, *before)


def swap(value, axis):
    size = lax.axis_size(axis)
    if size == 1:
        return jnp.zeros_like(value)
    return lax.ppermute(value, axis, [(i, i ^ 1) for i in range(size)])


def sum_over(value, axis):
    size = lax.axis_size(axis)
    if size & (size - 1):
        return lax.psum(value, axis)
    step = 1
    while step < size:
        other = lax.ppermute(value, axis, [(i, i ^ step) for i in range(size)])
        value = value + other
        step *= 2
    return value


def ring_order(count):
    return list(range(0, count, 2)) + list(range(1, count, 2))[::-1]


class Ring:
    def __init__(self, axis, width):
        self.axis = axis
        size = lax.axis_size(axis)
        self.count = size // 2
        order = ring_order(self.count)
        place = [order.index(chip) for chip in range(self.count)]
        me = lax.axis_index(axis)
        core = me % 2
        pos = jnp.asarray(place, jnp.int32)[me // 2]
        self.up = [(order[p] * 2 + c, order[(p + 1) % self.count] * 2 + c) for p in range(self.count) for c in (0, 1)]
        self.down = [(dst, src) for src, dst in self.up]
        self.block = width // size
        row = lax.broadcasted_iota(jnp.int32, (self.count, self.block, width), 0)
        off = lax.broadcasted_iota(jnp.int32, (self.count, self.block, width), 1)
        col = lax.broadcasted_iota(jnp.int32, (self.count, self.block, width), 2)
        self.firsts = sorted({0, max(self.count - 2, 0)})
        self.blocks = self.firsts + [m for m in range(self.count) if m not in self.firsts]
        turn = jnp.asarray(self.blocks, jnp.int32)
        chips = jnp.asarray(order, jnp.int32)[(pos - 1 - turn) % self.count]
        start = chips[:, None, None] * (2 * self.block) + off
        shape = (self.count * self.block, width)
        picks = [(col == start + side * self.block).reshape(shape) for side in (core, 1 - core)]
        self.pick = jnp.concatenate(picks, axis=0).astype(bf16)

    def rows(self, source):
        both = matmul_nt(self.pick, source)
        return both, swap(both[both.shape[0] // 2 :], self.axis)

    def reduce(self, partials):
        n, half = self.count, self.block // 2
        where = {}
        for arr in partials:
            for row in range(0, arr.shape[0], self.block):
                where[self.blocks[len(where)]] = (arr, row)

        def part(m, way):
            arr, row = where[m]
            return arr[row + way * half : row + (way + 1) * half]

        if n == 1:
            return partials[0]
        going, coming = part(0, 0), part(n - 2, 1)
        for step in range(n - 1):
            going = lax.ppermute(going, self.axis, self.up)
            coming = lax.ppermute(coming, self.axis, self.down)
            going = going + part(step + 1, 0)
            coming = coming + part((n - 3 - step) % n, 1)
        return jnp.concatenate([going, coming], axis=0)


def grads_kernel(row_of, starts, counts, *refs):
    pairs = max(row_of) + 1
    row_refs, refs = refs[: 2 * pairs], refs[2 * pairs :]
    own_refs, sent_refs = refs[: len(row_of)], refs[len(row_of) : -3]
    out_ref, rows_ref, cols_ref = refs[-3:]
    step = pl.program_id(0)
    depth = row_refs[0].shape[1]

    @pl.when(step == 0)
    def _():
        for pair in range(pairs):
            rows_ref[pair, :, :depth] = row_refs[2 * pair][...].astype(bf16)
            rows_ref[pair, :, depth:] = row_refs[2 * pair + 1][...].astype(bf16)

    chosen = 0
    for index, pair in enumerate(row_of):
        here = (step >= starts[index]) & (step < starts[index] + counts[index])
        chosen = chosen + jnp.where(here, pair, 0)

        @pl.when(here)
        def _(index=index):
            cols_ref[:depth] = own_refs[index][...].astype(bf16)
            cols_ref[depth:] = sent_refs[index][...].astype(bf16)

    out_ref[...] = jnp.dot(rows_ref[chosen], cols_ref[...], preferred_element_type=f32)


def weight_grads(rows, cols, height):
    widths = [width for *_, width in cols]
    tile = math.gcd(*widths, *[first for *_, first, _ in cols])
    tile = 512 if tile % 512 == 0 else tile
    counts = [width // tile for width in widths]
    starts = [sum(counts[:i]) for i in range(len(counts))]
    flat_rows = [arr for pair in rows for arr in pair]
    depth = flat_rows[0].shape[1]

    def col_spec(start, span, first):
        return pl.BlockSpec((depth, tile), lambda j: (0, first + jnp.clip(j - start, 0, span - 1)))

    firsts = [first // tile for *_, first, _ in cols]
    col_specs = [col_spec(*places) for places in zip(starts, counts, firsts)]
    return pl.pallas_call(
        functools.partial(grads_kernel, tuple(pair for pair, *_ in cols), tuple(starts), tuple(counts)),
        grid=(sum(counts),),
        in_specs=[pl.BlockSpec((height, depth), lambda j: (0, 0)) for _ in flat_rows] + col_specs * 2,
        out_specs=pl.BlockSpec((height, tile), lambda j: (0, j)),
        out_shape=jax.ShapeDtypeStruct((height, sum(widths)), f32),
        scratch_shapes=[
            pltpu.VMEM((len(rows), height, 2 * depth), bf16),
            pltpu.VMEM((2 * depth, tile), bf16),
        ],
    )(*flat_rows, *[col[1] for col in cols], *[col[2] for col in cols])


def layer(
    inputs,
    cotangent,
    lengths,
    norm1_gain,
    w_query,
    w_key,
    w_value,
    w_gate,
    w_alpha,
    w_beta,
    conv_query,
    conv_key,
    conv_value,
    a_log,
    dt_bias,
    onorm_gain,
    w_out,
    norm2_gain,
    w_one,
    w_three,
    w_two,
):
    seq_count, seq_len, width_d = inputs.shape
    row_count = seq_count * seq_len
    heads = a_log.shape[0]
    ring = Ring(DP, width_d)

    positions = lax.broadcasted_iota(jnp.int32, (seq_count, seq_len), 1)
    live_rows = (positions < lengths[:, None]).astype(f32).reshape(row_count, 1)
    x_rows = inputs.reshape(row_count, width_d).astype(f32)
    h_one = rms_scale(x_rows, norm1_gain).astype(bf16)
    w_ab = jnp.concatenate([w_alpha, w_beta], axis=1)
    matrices = (w_query, w_key, w_value, w_gate, w_ab)
    raws = tuple(
        jnp.dot(h_one, matrix, preferred_element_type=f32).astype(bf16) for matrix in matrices
    )
    arrays = raws + (
        conv_query,
        conv_key,
        conv_value,
        a_log.reshape(1, heads),
        dt_bias.reshape(1, heads),
        onorm_gain.reshape(1, -1),
    )
    gated_out, gated_trade, *saved = mixer_forward(heads, seq_len, arrays)
    mixed = jnp.dot(gated_out, w_out, preferred_element_type=f32)
    x_mid = x_rows + (mixed + swap(mixed, TENSOR))

    grad_out = cotangent.reshape(row_count, width_d).astype(f32) * live_rows
    grad_out_b = grad_out.astype(bf16)
    d_hidden = matmul_nt(grad_out_b, w_two)
    rows_out = ring.rows(grad_out_b)
    rows_one = ring.rows(h_one)
    gated_sent = swap(gated_trade, DP)

    h_two = rms_scale(x_mid, norm2_gain).astype(bf16)
    pre_one = jnp.dot(h_two, w_one, preferred_element_type=f32)
    pre_three = jnp.dot(h_two, w_three, preferred_element_type=f32)
    sig_one = jax.nn.sigmoid(pre_one)
    hidden = (pre_one * sig_one * pre_three).astype(bf16)
    d_pre_one = (d_hidden * pre_three * sig_one * (1.0 + pre_one * (1.0 - sig_one))).astype(bf16)
    d_pre_three = (d_hidden * pre_one * sig_one).astype(bf16)
    d_h_two = matmul_nt(d_pre_one, w_one) + matmul_nt(d_pre_three, w_three)
    d_h_two = d_h_two + swap(d_h_two, TENSOR)

    rows_two = ring.rows(h_two)
    ffn_cols = (d_pre_one, d_pre_three, hidden)
    ffn_sent = [swap(arr.astype(f32), DP) for arr in ffn_cols]
    tall = rows_two[1].shape[0]
    ffn_grads = [(pair, own, sent, 0, own.shape[1]) for pair, own, sent in zip((0, 0, 1), ffn_cols, ffn_sent)]
    ffn_partial = weight_grads((rows_two, rows_out), ffn_grads, tall)
    ffn_sum = ring.reduce([ffn_partial])

    ffn_out = jnp.dot(hidden, w_two, preferred_element_type=f32)
    ffn_other = swap(ffn_out, TENSOR)

    _, norm2_back = jax.vjp(rms_scale, x_mid, norm2_gain)
    d_mid_part, grad_norm2 = norm2_back(d_h_two)
    d_x_mid = grad_out + d_mid_part
    d_mid_b = d_x_mid.astype(bf16)
    d_gated = matmul_nt(d_mid_b, w_out)
    rows_mid = ring.rows(d_mid_b)
    weights = (*matrices[:4], jnp.transpose(w_ab).astype(f32))
    sums, trades, convs = None, [], []
    for part in range(PARTS):
        back = mixer_backward(part, PARTS, heads, seq_len, arrays, saved, d_gated, weights, sums)
        sums = back[:4]
        trades.append((back[4], swap(back[4], DP)))
        convs.append([jnp.sum(conv, axis=0) for conv in back[5:]])
    d_h_part, d_ab, g_small, g_onorm = sums

    x_late, ffn_late, d_ab = lax.optimization_barrier((x_mid, ffn_out, d_ab))
    outputs = ((x_late + (ffn_late + ffn_other)) * live_rows).reshape(seq_count, seq_len, width_d)

    d_h_one = d_h_part + swap(d_h_part, TENSOR)
    g_onorm = g_onorm + swap(g_onorm, TENSOR)
    _, norm1_back = jax.vjp(rms_scale, x_rows, norm1_gain)
    d_in_part, grad_norm1 = norm1_back(d_h_one)
    in_grad = (d_x_mid + d_in_part).reshape(seq_count, seq_len, width_d)

    wide = gated_out.shape[1] // PARTS
    mixer_sums = []
    for part, (own, sent) in enumerate(trades):
        cols = [(0, own, sent, 0, own.shape[1]), (1, gated_out, gated_sent, part * wide, wide)]
        partial = weight_grads((rows_one, rows_mid), cols, tall)
        mixer_sums.append(ring.reduce([partial]))

    g_ab = lax.dot_general(d_ab.astype(bf16), h_one, (((0,), (0,)), ((), ())), preferred_element_type=f32)
    g_convs = [conv for part in convs for conv in part]
    small_parts = (grad_norm1, grad_norm2, g_onorm, g_small, g_ab, *g_convs)
    sizes = [part.size // LANES for part in small_parts]
    packed = jnp.concatenate([part.reshape(-1, LANES) for part in small_parts], axis=0)
    packed = sum_over(packed, DP)
    unpacked, offset = [], 0
    for part, size in zip(small_parts, sizes):
        unpacked.append(packed[offset : offset + size].reshape(part.shape))
        offset = offset + size
    grad_norm1, grad_norm2, g_onorm, g_small, g_ab = unpacked[:5]
    g_conv_q, g_conv_k, g_conv_v = (jnp.concatenate(unpacked[5 + i :: 3], axis=1) for i in range(3))
    block = width_d // lax.axis_size(DP)
    g_ab = lax.dynamic_slice_in_dim(g_ab, lax.axis_index(DP) * block, block, axis=1).T

    sizes = [matrix.shape[1] // heads for matrix in matrices[:4]]
    span = sum(sizes)
    heads_end = heads // PARTS * span
    pieces = []
    for index, size in enumerate(sizes):
        start = sum(sizes[:index])
        cols = [total[:, at + start : at + start + size] for total in mixer_sums for at in range(0, heads_end, span)]
        pieces.append(jnp.concatenate(cols, axis=1))
    pieces.append(jnp.concatenate([total[:, heads_end:] for total in mixer_sums], axis=1))
    ff_local = w_one.shape[1]
    return (
        outputs,
        in_grad,
        grad_norm1,
        pieces[0],
        pieces[1],
        pieces[2],
        pieces[3],
        g_ab[:, :heads],
        g_ab[:, heads:],
        g_conv_q,
        g_conv_k,
        g_conv_v,
        g_small[0, :heads],
        g_small[1, :heads],
        g_onorm.reshape(-1),
        jnp.transpose(pieces[4]),
        grad_norm2,
        ffn_sum[:, :ff_local],
        ffn_sum[:, ff_local : 2 * ff_local],
        jnp.transpose(ffn_sum[:, 2 * ff_local :]),
    )


def solution(mesh):
    in_specs = (
        P(DP, None, None),
        P(DP, None, None),
        P(DP),
        P(),
        P(None, TENSOR),
        P(None, TENSOR),
        P(None, TENSOR),
        P(None, TENSOR),
        P(None, TENSOR),
        P(None, TENSOR),
        P(None, TENSOR),
        P(None, TENSOR),
        P(None, TENSOR),
        P(TENSOR),
        P(TENSOR),
        P(),
        P(TENSOR, None),
        P(),
        P(None, TENSOR),
        P(None, TENSOR),
        P(TENSOR, None),
    )
    out_specs = (
        P(DP, None, None),
        P(DP, None, None),
        P(),
        P(DP, TENSOR),
        P(DP, TENSOR),
        P(DP, TENSOR),
        P(DP, TENSOR),
        P(DP, TENSOR),
        P(DP, TENSOR),
        P(None, TENSOR),
        P(None, TENSOR),
        P(None, TENSOR),
        P(TENSOR),
        P(TENSOR),
        P(),
        P(TENSOR, DP),
        P(),
        P(DP, TENSOR),
        P(DP, TENSOR),
        P(TENSOR, DP),
    )
    return jax.shard_map(layer, mesh=mesh, in_specs=in_specs, out_specs=out_specs, check_vma=False)
```
